512 devices in a mesh: layer: 16 (over z, core), plane: 32 (over x, y).
Axes of the slice: x: 4, y: 8, z: 8, core: 2. Of those that a mesh axis runs over, the one named last changes fastest.
Arguments:
- velocity: bfloat16 [2, 128, 131072], P(None, 'layer', 'plane'), may hold values from -6 to 6
- adjoint: bfloat16 [2, 128, 131072], P(None, 'layer', 'plane'), may hold values from -6 to 6
- corners: int32 [4, 131072], P(None, 'plane'), may hold values from 0 to 4607, as said below
- shared: int32 [4, 4096], P(None, 'plane'), may hold values from 0 to 4096, as said below
- stretch: float32 [2, 131072], P(None, 'plane'), may hold values from 0.5 to 2
- shear_part: float32 [2, 131072], P(None, 'plane'), may hold values from -0.2 to 0.2
- thickness: float32 [128, 131072], P('layer', 'plane'), may hold values from 0.3 to 3
- rate_factor: float32 [128, 131072], P('layer', 'plane'), may hold values from 0.5 to 2
- retention: float32 [128, 131072], P('layer', 'plane'), may hold values from 0.2 to 1
- weight: float32 [128, 131072], P('layer', 'plane'), may hold values from 0.5 to 2
Outputs:
- gradient: float32 [131072], P('plane')
The draws below stay inside these ranges and needn't reach their ends.
Inputs may be any that keep to these rules, and one draw needn't show every extreme that they name: `corners`: below 4096 a number names an owned node; 4096 + j * 128 + s names slot s of the ghost block of direction j (plane offsets -2, -1, +1, +2). Every slot of a block whose partition exists is named by exactly one corner, corner 0 of some element; blocks of directions beyond the ends of the plane axis are named by none. `shared`: row j, block p lists 128 distinct owned nodes of partition p that the partition at offset o_j (-2, -1, +1, +2) holds as ghosts; the block is 4096 throughout where that partition does not exist.
All inputs are finite; a program needn't handle non-finite values.
Results may differ from the reference program's by a relative error of at most 0.0003.
Values may be sent and summed in bfloat16 or wider, within the bound.
A program may use at most 128 MiB of HBM per device.

```python
import math
import jax
import jax.numpy as jnp
from jax import lax

ELEM_DEV = 4096
SLOT = 128
NOWN = 4096
LAYER_TOTAL = 128
ELEMS = 131072
NODES = 131072
N_PLANE = 32


OFFSETS = (-2, -1, 1, 2)


def direction_valid():
    owners = jnp.arange(N_PLANE, dtype=jnp.int32)
    offset_list = jnp.array(OFFSETS, dtype=jnp.int32)
    source = owners[:, None] + offset_list[None, :]
    return (source >= 0) & (source < N_PLANE)


def draw_shared(key, part):

    def one_list(list_index):
        return jax.random.permutation(jax.random.fold_in(key, list_index), NOWN)[:SLOT].astype(jnp.int32)
    lists = jax.vmap(one_list)(jnp.arange(N_PLANE * 4, dtype=jnp.int32))
    lists = lists.reshape(N_PLANE, 4, SLOT)
    valid_mask = direction_valid()
    lists = jnp.where(valid_mask[:, :, None], lists, NOWN)
    return jnp.transpose(lists, (1, 0, 2)).reshape(4, N_PLANE * SLOT).astype(jnp.int32)


def draw_corners(key, part):
    key_base = jax.random.fold_in(key, 11)
    key_perm = jax.random.fold_in(key, 12)
    base_nodes = jax.random.randint(key_base, (4, N_PLANE, ELEM_DEV), 0, NOWN, dtype=jnp.int32)

    def one_perm(plane_index):
        return jax.random.permutation(jax.random.fold_in(key_perm, plane_index), ELEM_DEV)[:4 * SLOT].astype(jnp.int32)
    places = jax.vmap(one_perm)(jnp.arange(N_PLANE, dtype=jnp.int32))
    slot_ids = jnp.arange(4 * SLOT, dtype=jnp.int32)
    valid_mask = direction_valid()[:, slot_ids // SLOT]
    plane_rows = jnp.broadcast_to(jnp.arange(N_PLANE, dtype=jnp.int32)[:, None], places.shape)
    first_corner = base_nodes[0]
    current = first_corner[plane_rows, places]
    chosen = jnp.where(valid_mask, NOWN + slot_ids[None, :], current).astype(jnp.int32)
    first_corner = first_corner.at[plane_rows, places].set(chosen)
    base_nodes = base_nodes.at[0].set(first_corner)
    return base_nodes.reshape(4, N_PLANE * ELEM_DEV).astype(jnp.int32)


def draw_retention(key, part):
    random_key_sequence = [jax.random.fold_in(key, 21 + offset_index) for offset_index in range(6)]
    lattice_shape = (LAYER_TOTAL, ELEMS)
    slow_share = 0.5
    slow_mask = jax.random.bernoulli(random_key_sequence[0], slow_share, (1, ELEMS))
    total_keep = jnp.exp(jax.random.uniform(random_key_sequence[1], (1, ELEMS), jnp.float32, math.log(0.5), math.log(0.9)))
    layer_factor = jnp.exp(jax.random.uniform(random_key_sequence[2], (LAYER_TOTAL, 1), jnp.float32, math.log(0.5), math.log(1.5)))
    constant_flow_rate = jnp.exp(jnp.log(total_keep) * layer_factor / LAYER_TOTAL)
    sudden_event_mask = jax.random.bernoulli(random_key_sequence[3], 2.0 / LAYER_TOTAL, lattice_shape)
    sudden_keep_flag = jax.random.uniform(random_key_sequence[4], lattice_shape, jnp.float32, 0.5, 0.8)
    gentle_flow_rate = jnp.where(sudden_event_mask, constant_flow_rate * sudden_keep_flag, constant_flow_rate)
    fast_rate = jax.random.uniform(random_key_sequence[5], lattice_shape, jnp.float32, 0.2, 0.6)
    return jnp.where(slow_mask, gentle_flow_rate, fast_rate).astype(jnp.float32)


def levels(rng, shape, split, low, largest):
    gain = 1.0
    for axis_at, blocks in split:
        heights = jax.random.uniform(jax.random.fold_in(jax.random.fold_in(rng, 6), axis_at), (blocks,), jnp.float32, low / len(split), largest / len(split))
        gain = gain * jnp.repeat(jnp.exp(heights), shape[axis_at] // blocks).reshape((-1,) + (1,) * (len(shape) - 1 - axis_at))
    return gain


def centred(own_key, extent, scale, most, shards=(), held_as=jnp.bfloat16):
    loudness = levels(own_key, extent, shards, -0.22, 0.18) if shards else 1.0
    result = jax.random.normal(own_key, extent, jnp.float32) * scale * loudness
    return jnp.minimum(jnp.maximum(result, -most), most).astype(held_as)


def setup_inputs(seed: int = 0) -> dict:
    arg_keys = jax.random.split(jax.random.key(seed), 11)
    return {
        "velocity": centred(arg_keys[0], (2, LAYER_TOTAL, NODES), 1.0, 6.0, ((1, 16), (2, 32))),
        "adjoint": centred(arg_keys[1], (2, LAYER_TOTAL, NODES), 1.0, 6.0, ((1, 16), (2, 32))),
        "corners": draw_corners(jax.random.fold_in(arg_keys[10], 71), 0),
        "shared": draw_shared(jax.random.fold_in(arg_keys[10], 71), 0),
        "stretch": jnp.clip(jnp.exp(math.log(2.0) - 1.3862944 * jax.random.uniform(arg_keys[4], (2, ELEMS), jnp.float32) ** levels(arg_keys[4], (2, ELEMS), ((1, 32),), -0.2, 0.2)), 0.5, 2.0),
        "shear_part": jnp.clip(jax.random.uniform(arg_keys[5], (2, ELEMS), jnp.float32, -0.2, 0.2) * levels(arg_keys[5], (2, ELEMS), ((1, 32),), -0.4, 0.0), -0.2, 0.2),
        "thickness": jnp.clip(jnp.exp(math.log(3.0) - 2.3025851 * jax.random.uniform(arg_keys[6], (LAYER_TOTAL, ELEMS), jnp.float32) ** levels(arg_keys[6], (LAYER_TOTAL, ELEMS), ((0, 16), (1, 32)), -0.2, 0.2)), 0.3, 3.0),
        "rate_factor": jnp.clip(jnp.exp(math.log(2.0) - 1.3862944 * jax.random.uniform(arg_keys[7], (LAYER_TOTAL, ELEMS), jnp.float32) ** levels(arg_keys[7], (LAYER_TOTAL, ELEMS), ((0, 16), (1, 32)), -0.2, 0.2)), 0.5, 2.0),
        "retention": draw_retention(jax.random.fold_in(arg_keys[10], 71), 0),
        "weight": jnp.clip(jnp.exp(math.log(2.0) - 1.3862944 * jax.random.uniform(arg_keys[9], (LAYER_TOTAL, ELEMS), jnp.float32) ** levels(arg_keys[9], (LAYER_TOTAL, ELEMS), ((0, 16), (1, 32)), -0.2, 0.2)), 0.5, 2.0),
    }


OFFSETS = (-2, -1, 1, 2)
STRAIN_EPS = 0.01

def basis_table():
    gauss_point = 1.0 / math.sqrt(3.0)
    xi_signs = [-1.0, 1.0, 1.0, -1.0, -1.0, 1.0, 1.0, -1.0]
    eta_signs = [-1.0, -1.0, 1.0, 1.0, -1.0, -1.0, 1.0, 1.0]
    zeta_signs = [1.0, 1.0, 1.0, 1.0, -1.0, -1.0, -1.0, -1.0]
    shape_table = [[0.0] * 8 for row_index in range(24)]
    for point_index in range(8):
        xi_point = gauss_point if point_index & 1 else -gauss_point
        eta_point = gauss_point if point_index & 2 else -gauss_point
        zeta_point = gauss_point if point_index & 4 else -gauss_point
        for node_index in range(8):
            along_xi = 1.0 + xi_signs[node_index] * xi_point
            along_eta = 1.0 + eta_signs[node_index] * eta_point
            along_zeta = 1.0 + zeta_signs[node_index] * zeta_point
            shape_table[point_index][node_index] = xi_signs[node_index] * along_eta * along_zeta / 8.0
            shape_table[8 + point_index][node_index] = eta_signs[node_index] * along_xi * along_zeta / 8.0
            shape_table[16 + point_index][node_index] = zeta_signs[node_index] * along_xi * along_eta / 8.0
    return shape_table

def strain_of(grad_x, grad_y, grad_z, first_comp, second_comp):
    return (grad_x[first_comp], grad_y[second_comp], 0.5 * (grad_y[first_comp] + grad_x[second_comp]), 0.5 * grad_z[first_comp], 0.5 * grad_z[second_comp])

def pairing(left_strain, right_strain):
    return left_strain[0] * right_strain[0] + left_strain[1] * right_strain[1] + 0.5 * (left_strain[0] * right_strain[1] + left_strain[1] * right_strain[0]) + left_strain[2] * right_strain[2] + left_strain[3] * right_strain[3] + left_strain[4] * right_strain[4]

def element_terms(nodal_values, stretch, shear_part, thickness, rate_factor):
    layer_count = nodal_values.shape[1] - 1
    width = nodal_values.shape[3]
    top_nodes = nodal_values[:, :-1]
    bottom_nodes = nodal_values[:, 1:]
    hexa_nodes = jnp.concatenate([top_nodes, bottom_nodes], axis=2)
    basis = jnp.asarray(basis_table(), dtype=jnp.float32)
    derived = jnp.einsum('rn,clnb->clrb', basis, hexa_nodes, precision=lax.Precision.HIGHEST)
    derived = derived.reshape(4, layer_count, 3, 8, width)
    along_xi = derived[:, :, 0]
    along_eta = derived[:, :, 1]
    along_zeta = derived[:, :, 2]
    grad_x = stretch[0] * along_xi + shear_part[0] * along_eta
    grad_y = shear_part[1] * along_xi + stretch[1] * along_eta
    grad_z = (2.0 / thickness)[None, :, None, :] * along_zeta
    flow_strain = strain_of(grad_x, grad_y, grad_z, 0, 1)
    adjoint_strain = strain_of(grad_x, grad_y, grad_z, 2, 3)
    effective = pairing(flow_strain, flow_strain) + STRAIN_EPS
    viscosity = 0.5 * rate_factor[:, None, :] * jnp.power(effective, -1.0 / 3.0)
    volume = 0.5 * thickness / (stretch[0] * stretch[1] - shear_part[0] * shear_part[1])
    return volume * lax.optimization_barrier(jnp.sum(4.0 * viscosity * pairing(flow_strain, adjoint_strain), axis=1))

def reference(velocity, adjoint, corners, shared, stretch, shear_part, thickness, rate_factor, retention, weight):
    fields = jnp.concatenate([velocity, adjoint], axis=0).astype(jnp.float32)
    fields = jnp.concatenate([fields, jnp.zeros((4, 1, NODES), jnp.float32)], axis=1)
    ghost_pos = jnp.arange(4 * SLOT, dtype=jnp.int32)
    direction = ghost_pos // SLOT
    slot_pos = ghost_pos % SLOT
    offset_of = jnp.array(OFFSETS, dtype=jnp.int32)[direction]
    owners = jnp.arange(N_PLANE, dtype=jnp.int32)
    source = owners[:, None] + offset_of[None, :]
    valid_mask = (source >= 0) & (source < N_PLANE)
    safe_source = jnp.clip(source, 0, N_PLANE - 1)
    owned_at = shared[(3 - direction)[None, :], safe_source * SLOT + slot_pos[None, :]]
    ghost_global = jnp.where(valid_mask, safe_source * NOWN + owned_at, 0).astype(jnp.int32)
    own_global = owners[:, None] * NOWN + jnp.arange(NOWN, dtype=jnp.int32)[None, :]
    global_table = jnp.concatenate([own_global, ghost_global], axis=1)
    plane_of = jnp.arange(ELEMS, dtype=jnp.int32) // ELEM_DEV
    global_corners = global_table[plane_of[None, :], corners].astype(jnp.int32)
    block_size = min(1024, ELEM_DEV)
    block_count = ELEMS // block_size

    def one_block(block_start):
        corner_ids = lax.dynamic_slice_in_dim(global_corners, block_start, block_size, 1)
        nodal_values = jnp.take(fields, corner_ids, axis=2)
        return element_terms(nodal_values, lax.dynamic_slice_in_dim(stretch, block_start, block_size, 1), lax.dynamic_slice_in_dim(shear_part, block_start, block_size, 1), lax.dynamic_slice_in_dim(thickness, block_start, block_size, 1), lax.dynamic_slice_in_dim(rate_factor, block_start, block_size, 1))
    starts = jnp.arange(block_count, dtype=jnp.int32) * block_size
    layer_terms = lax.map(one_block, starts)
    layer_terms = jnp.transpose(layer_terms, (1, 0, 2)).reshape(LAYER_TOTAL, ELEMS)

    def layer_step(running, inputs):
        keep_share, layer_weight, layer_term = inputs
        running_next = keep_share * running + (1.0 - keep_share) * layer_weight
        return (running_next, running_next * layer_term)
    _, weighted = lax.scan(layer_step, jnp.zeros((ELEMS,), jnp.float32), (retention, weight, layer_terms))
    column = lax.optimization_barrier(jnp.sum(weighted, axis=0))
    spread = jnp.tile(0.25 * column, 4)
    return jax.ops.segment_sum(spread, global_corners.reshape(-1), num_segments=NODES)
```

```python
import functools
import math

import jax
import jax.numpy as jnp
from jax import lax
from jax.experimental import pallas as pl
from jax.experimental.pallas import tpu as pltpu
from jax.sharding import PartitionSpec as P

OFFSETS = (-2, -1, 1, 2)
STRAIN_EPS = 0.01
GAUSS = 1.0 / math.sqrt(3.0)
MESH = pl.DeviceIdType.MESH
WIDE = 256
OWN_ROWS = 16
ALL_ROWS = 18
MAIN_BLOCK = 512
SCATTER_BLOCK = 1024


def iota(shape, axis):
    return lax.broadcasted_iota(jnp.int32, shape, axis)


def one_hot(low, width):
    return (iota((width, low.shape[1]), 0) == low).astype(jnp.float32).astype(jnp.bfloat16)


def pick(row, size, table, count):
    out = table[0:size]
    for i in range(1, count):
        out = jnp.where(row == i, table[i * size : (i + 1) * size], out)
    return out


def corner_modes(v):
    p, q, r, s = v[1] - v[0], v[2] - v[3], v[0] + v[1], v[2] + v[3]
    return r + s, p + q, s - r, q - p


def element_terms(upper, lowest, stretch, shear, thick, rate):
    n = thick.shape[1]
    last = iota((8, n), 0) == 7
    top, end = corner_modes(upper), corner_modes(lowest)
    derived = []
    for comp in range(4):
        half, diff = [], []
        for m in range(4):
            t = top[m][comp * 8 : (comp + 1) * 8]
            b = jnp.where(last, pltpu.roll(end[m], 7 - comp, 0), pltpu.roll(t, 7, 0))
            d = t - b
            diff.append(d)
            if m:
                mean = t + b
                gd = GAUSS * d
                half.append((mean - gd, mean + gd))
        mx, my, mxy = half
        xi, eta = [], []
        for z in range(2):
            t = GAUSS * mxy[z]
            xi.append((mx[z] - t, mx[z] + t))
            eta.append((my[z] - t, my[z] + t))
        d0, dx, dy, dxy = diff
        gx, gy, gxy = GAUSS * dx, GAUSS * dy, (GAUSS * GAUSS) * dxy
        a0, a1, b0, b1 = d0 - gx, d0 + gx, gy - gxy, gy + gxy
        derived.append((xi, eta, ((a0 - b0, a0 + b0), (a1 - b1, a1 + b1))))
    s0, s1 = 0.125 * stretch[0:1], 0.125 * stretch[1:2]
    h0, h1 = 0.125 * shear[0:1], 0.125 * shear[1:2]
    inv = 0.125 / thick

    def strains(first, second):
        axi, aeta, az = derived[first]
        bxi, beta, bz = derived[second]
        two = range(2)
        return (
            [[s0 * axi[z][e] for e in two] for z in two],
            [[h0 * aeta[z][x] for x in two] for z in two],
            [[h1 * bxi[z][e] for e in two] for z in two],
            [[s1 * beta[z][x] for x in two] for z in two],
            [[h1 * axi[z][e] + s0 * bxi[z][e] for e in two] for z in two],
            [[s1 * aeta[z][x] + h0 * beta[z][x] for x in two] for z in two],
            [[inv * az[x][e] for e in two] for x in two],
            [[inv * bz[x][e] for e in two] for x in two],
        )

    f, g = strains(0, 1), strains(2, 3)
    total = None
    for x in range(2):
        for e in range(2):
            fxz, fyz, gxz, gyz = f[6][x][e], f[7][x][e], g[6][x][e], g[7][x][e]
            own_z = fxz * fxz + fyz * fyz + STRAIN_EPS
            cross_z = fxz * gxz + fyz * gyz
            for z in range(2):
                fxx, fyy = f[0][z][e] + f[1][z][x], f[2][z][e] + f[3][z][x]
                fxy = 0.5 * (f[4][z][e] + f[5][z][x])
                gxx, gyy = g[0][z][e] + g[1][z][x], g[2][z][e] + g[3][z][x]
                gxy = 0.5 * (g[4][z][e] + g[5][z][x])
                a, b = fxx + 0.5 * fyy, fyy + 0.5 * fxx
                effective = fxx * a + fyy * b + fxy * fxy + own_z
                cross = gxx * a + gyy * b + fxy * gxy + cross_z
                term = jnp.exp2((-1.0 / 3.0) * jnp.log2(effective)) * cross
                total = term if total is None else total + term
    det = stretch[0:1] * stretch[1:2] - shear[0:1] * shear[1:2]
    return (rate * thick) * (total / det)


def recurrence(keep, wei):
    sub = iota(keep.shape, 0)
    factor, offset = keep, (1.0 - keep) * wei
    for d in (1, 2, 4):
        before_f = jnp.where(sub >= d, pltpu.roll(factor, d, 0), 1.0)
        before_o = jnp.where(sub >= d, pltpu.roll(offset, d, 0), 0.0)
        offset = factor * before_o + offset
        factor = factor * before_f
    return factor, offset


def split_bf16(x):
    high = x.astype(jnp.bfloat16).astype(jnp.float32)
    return high, x - high


def kernel(
    layers,
    planes,
    vel_hbm, adj_hbm, cor_hbm, sha_hbm, str_hbm, she_hbm, thi_hbm, rat_hbm, ret_hbm, wei_hbm,
    out,
    vel, adj, corners, shared, stretch, shear, thick, rate, ret, wei,
    table, table8, low_send, low_own, gsend, grecv, lsend, lrecv,
    fac, off, sc_send, sc_recv, en_send, en_recv,
    abuf, bbuf, acc,
    rs_send, rs_recv, gh_send, gh_recv, ag_send, ag_recv,
    in_sem, low_s, low_r, g_s, g_r, l_s, l_r, sc_s, sc_r, en_s, en_r, rs_s, rs_r, gh_s, gh_r, ag_s, ag_r,
):
    g, p = lax.axis_index("layer"), lax.axis_index("plane")
    per = OWN_ROWS // layers
    f32, bf16 = jnp.float32, jnp.bfloat16

    hbm = (vel_hbm, adj_hbm, sha_hbm, ret_hbm, wei_hbm, cor_hbm, str_hbm, she_hbm, thi_hbm, rat_hbm)
    own = (vel, adj, shared, ret, wei, corners, stretch, shear, thick, rate)
    loads = [pltpu.make_async_copy(a, b, in_sem.at[i]) for i, (a, b) in enumerate(zip(hbm, own))]
    for load in loads:
        load.start()

    valid = [jnp.logical_and(p + o >= 0, p + o < planes) for o in OFFSETS]
    up, down = g > 0, g < layers - 1

    for d in range(4):
        @pl.when(jnp.logical_not(valid[d]))
        def _():
            grecv[d] = jnp.zeros(grecv.shape[1:], bf16)
            lrecv[d] = jnp.zeros(lrecv.shape[1:], bf16)
            gh_recv[d] = jnp.zeros(gh_recv.shape[1:], f32)

    @pl.when(jnp.logical_not(down))
    def _():
        low_own[...] = jnp.zeros(low_own.shape, bf16)
        lrecv[...] = jnp.zeros(lrecv.shape, bf16)

    barrier = pltpu.get_barrier_semaphore()

    def greet(layer, plane):
        pl.semaphore_signal(barrier, inc=1, device_id=(layer, plane), device_id_type=MESH)

    def greet_layer(r, _):
        greet(lax.rem(g + r, layers), p)
        return 0

    lax.fori_loop(1, layers, greet_layer, 0)
    expected = layers - 1
    for d, o in enumerate(OFFSETS):
        @pl.when(valid[d])
        def _():
            greet(g, p + o)

        @pl.when(jnp.logical_and(valid[d], up))
        def _():
            greet(g - 1, p + o)

        @pl.when(jnp.logical_and(valid[d], down))
        def _():
            greet(g + 1, p + o)

        expected = expected + valid[d].astype(jnp.int32) * (1 + up.astype(jnp.int32) + down.astype(jnp.int32))

    loads[0].wait()
    loads[1].wait()
    for i in range(OWN_ROWS):
        at = slice(i * WIDE, (i + 1) * WIDE)
        table[i * 32 : (i + 1) * 32] = jnp.concatenate(
            [vel[0, :, at], vel[1, :, at], adj[0, :, at], adj[1, :, at]], axis=0
        )
    row8 = iota((8, WIDE), 0)
    pieces = []
    for i in range(0, OWN_ROWS, 2):
        piece = jnp.zeros((8, WIDE), f32)
        for half in range(2):
            for comp in range(4):
                level = (vel, adj)[comp // 2][comp % 2, :, (i + half) * WIDE : (i + half + 1) * WIDE].astype(f32)
                piece = jnp.where(row8 == half * 4 + comp, level[0:1], piece)
        pieces.append(piece)
    low_send[...] = jnp.concatenate(pieces, axis=0).astype(bf16)
    loads[2].wait()
    row16 = iota((16, 128), 0)
    for j in range(4):
        ids = shared[j : j + 1, :]
        sent = jnp.dot(table[0 : OWN_ROWS * 32], one_hot(ids & (WIDE - 1), WIDE), preferred_element_type=f32)
        sent = pick(ids >> 8, 32, sent, OWN_ROWS)
        gsend[j] = sent.astype(bf16)
        tops = jnp.zeros((16, 128), f32)
        for comp in range(4):
            tops = jnp.where(row16 == comp, sent[comp * 8 : comp * 8 + 1], tops)
        lsend[j] = tops.astype(bf16)
    loads[3].wait()
    loads[4].wait()
    for i in range(8):
        at = slice(i * 512, (i + 1) * 512)
        factor, offset = recurrence(ret[:, at], wei[:, at])
        fac[:, at] = factor
        off[:, at] = offset
    for i in range(layers):
        for k in range(per):
            at = slice((i * per + k) * WIDE, (i * per + k + 1) * WIDE)
            sc_send[i, k : k + 1, :] = fac[7:8, at]
            sc_send[i, per + k : per + k + 1, :] = off[7:8, at]

    pl.semaphore_wait(barrier, expected)

    def remote(src, dst, s, r, layer, plane):
        return pltpu.make_async_remote_copy(
            src_ref=src, dst_ref=dst, send_sem=s, recv_sem=r, device_id=(layer, plane), device_id_type=MESH
        )

    def to_all(send, recv, s, r, same=False):
        def copy(i):
            return remote(send if same else send.at[i], recv.at[g], s.at[i], r.at[g], i, p)

        def start(k, _):
            copy(lax.rem(g + k, layers)).start()
            return 0

        lax.fori_loop(1, layers, start, 0)

    def from_all(send, recv, s, r, same=False):
        def wait(k, _):
            i = lax.rem(g + k, layers)
            remote(send if same else send.at[i], recv.at[i], s.at[i], r.at[i], i, p).wait_recv()
            return 0

        lax.fori_loop(1, layers, wait, 0)

    def sent_all(send, recv, s, r, same=False):
        def wait(k, _):
            i = lax.rem(g + k, layers)
            remote(send if same else send.at[i], recv.at[i], s.at[i], r.at[i], i, p).wait_send()
            return 0

        lax.fori_loop(1, layers, wait, 0)

    def ghost(j):
        return remote(gsend.at[j], grecv.at[3 - j], g_s.at[j], g_r.at[3 - j], g, p + OFFSETS[j])

    def low_ghost(j):
        return remote(lsend.at[j], lrecv.at[3 - j], l_s.at[j], l_r.at[3 - j], g - 1, p + OFFSETS[j])

    low_copy = remote(low_send, low_own, low_s, low_r, g - 1, p)

    to_all(sc_send, sc_recv, sc_s, sc_r)
    for j in range(4):
        @pl.when(valid[j])
        def _():
            ghost(j).start()

        @pl.when(jnp.logical_and(valid[j], up))
        def _():
            low_ghost(j).start()

    @pl.when(up)
    def _():
        low_copy.start()

    sc_recv[g] = sc_send[g]
    from_all(sc_send, sc_recv, sc_s, sc_r)
    running = jnp.zeros((per, WIDE), f32)
    for i in range(layers):
        en_send[i] = running
        running = sc_recv[i, 0:per, :] * running + sc_recv[i, per : 2 * per, :]
    to_all(en_send, en_recv, en_s, en_r)
    en_recv[g] = en_send[g]

    for load in loads[5:]:
        load.wait()

    for j in range(4):
        @pl.when(valid[j])
        def _():
            remote(gsend.at[j], grecv.at[j], g_s.at[j], g_r.at[j], g, p + OFFSETS[j]).wait_recv()

        @pl.when(jnp.logical_and(valid[j], down))
        def _():
            remote(lsend.at[j], lrecv.at[j], l_s.at[j], l_r.at[j], g, p + OFFSETS[j]).wait_recv()

    @pl.when(down)
    def _():
        low_copy.wait_recv()

    for i in range(2):
        table[(OWN_ROWS + i) * 32 : (OWN_ROWS + i + 1) * 32] = jnp.concatenate([grecv[2 * i], grecv[2 * i + 1]], axis=1)
    table8[0:64] = low_own[...]
    first = jnp.concatenate([lrecv[0], lrecv[1]], axis=1).astype(f32)[0:8]
    second = jnp.concatenate([lrecv[2], lrecv[3]], axis=1).astype(f32)[0:8]
    ghosts8 = first + pltpu.roll(second, 4, 0)
    table8[64:80] = jnp.concatenate([ghosts8, jnp.zeros((8, WIDE), f32)], axis=0).astype(bf16)

    def main_block(b, _):
        at = pl.ds(pl.multiple_of(b * MAIN_BLOCK, MAIN_BLOCK), MAIN_BLOCK)
        upper, lowest = [], []
        for c in range(4):
            ids = corners[c : c + 1, at]
            row = ids >> 8
            hot = one_hot(ids & (WIDE - 1), WIDE)
            upper.append(pick(row, 32, jnp.dot(table[...], hot, preferred_element_type=f32), ALL_ROWS))
            both = pick(row >> 1, 8, jnp.dot(table8[...], hot, preferred_element_type=f32), ALL_ROWS // 2)
            lowest.append(jnp.where((row & 1) == 1, pltpu.roll(both, 4, 0), both))
        term = element_terms(upper, lowest, stretch[:, at], shear[:, at], thick[:, at], rate[:, at])
        abuf[:, at] = jnp.sum(fac[:, at] * term, axis=0, keepdims=True)
        bbuf[:, at] = jnp.sum(off[:, at] * term, axis=0, keepdims=True)
        return 0

    lax.fori_loop(0, corners.shape[1] // MAIN_BLOCK, main_block, 0)

    from_all(en_send, en_recv, en_s, en_r)
    for i in range(layers):
        for k in range(per):
            at = slice((i * per + k) * WIDE, (i * per + k + 1) * WIDE)
            abuf[:, at] = 0.25 * (abuf[:, at] * en_recv[i, k : k + 1, :] + bbuf[:, at])

    acc[...] = jnp.zeros(acc.shape, f32)

    def scatter_block(b, _):
        at = pl.ds(pl.multiple_of(b * SCATTER_BLOCK, SCATTER_BLOCK), SCATTER_BLOCK)
        row48 = iota((48, SCATTER_BLOCK), 0)
        high, low = split_bf16(abuf[:, at])
        value = jnp.where(row48 < 24, high, low)
        place = jnp.where(row48 < 24, row48, row48 - 24)
        out48 = None
        for c in range(4):
            ids = corners[c : c + 1, at]
            spread = jnp.where(place == (ids >> 8), value, 0.0).astype(bf16)
            part = lax.dot_general(
                one_hot(ids & (WIDE - 1), WIDE), spread, (((1,), (1,)), ((), ())), preferred_element_type=f32
            )
            out48 = part if out48 is None else out48 + part
        acc[...] += out48
        return 0

    lax.fori_loop(0, corners.shape[1] // SCATTER_BLOCK, scatter_block, 0)
    nodes = acc[...].T
    nodes = nodes[0:24] + nodes[24:48]
    for i in range(layers):
        for k in range(per):
            lo = i * per + k
            rs_send[i, 2 * k : 2 * k + 1, :] = nodes[lo : lo + 1, 0:128]
            rs_send[i, 2 * k + 1 : 2 * k + 2, :] = nodes[lo : lo + 1, 128:256]
    for j in range(4):
        gh_send[j] = nodes[OWN_ROWS + j // 2 : OWN_ROWS + j // 2 + 1, (j % 2) * 128 : (j % 2 + 1) * 128]

    def ghost_sum(j):
        return remote(gh_send.at[j], gh_recv.at[3 - j], gh_s.at[j], gh_r.at[3 - j], g, p + OFFSETS[j])

    for j in range(4):
        @pl.when(valid[j])
        def _():
            ghost_sum(j).start()
    to_all(rs_send, rs_recv, rs_s, rs_r)
    rs_recv[g] = rs_send[g]

    hots, spots = [], []
    row64 = iota((64, 128), 0) & 31
    for d in range(4):
        ids = shared[d : d + 1, :]
        hots.append(one_hot(ids & 127, 128))
        spots.append(row64 == (ids >> 7))

    for j in range(4):
        @pl.when(valid[j])
        def _():
            remote(gh_send.at[j], gh_recv.at[j], gh_s.at[j], gh_r.at[j], g, p + OFFSETS[j]).wait_recv()
    from_all(rs_send, rs_recv, rs_s, rs_r)
    total = rs_recv[0]
    for i in range(1, layers):
        total = total + rs_recv[i]
    ag_send[0 : 2 * per] = total
    for d in range(4):
        ag_send[2 * per + d : 2 * per + d + 1] = gh_recv[d]
    spare = ag_send.shape[0] - 2 * per - 4
    if spare:
        ag_send[2 * per + 4 :] = jnp.zeros((spare, 128), f32)
    to_all(ag_send, ag_recv, ag_s, ag_r, same=True)
    ag_recv[g] = ag_send[...]
    from_all(ag_send, ag_recv, ag_s, ag_r, same=True)

    arrived = ag_recv[0]
    for i in range(1, layers):
        arrived = arrived + ag_recv[i]
    result = jnp.concatenate([ag_recv[i, 0 : 2 * per, :] for i in range(layers)], axis=0)
    added = None
    half64 = iota((64, 128), 0) < 32
    for d in range(4):
        high, low = split_bf16(arrived[2 * per + d : 2 * per + d + 1])
        spread = jnp.where(spots[d], jnp.where(half64, high, low), 0.0).astype(bf16)
        part = lax.dot_general(spread, hots[d], (((1,), (1,)), ((), ())), preferred_element_type=f32)
        added = part if added is None else added + part
    out[...] = result + (added[0:32] + added[32:64])

    sent_all(sc_send, sc_recv, sc_s, sc_r)
    sent_all(en_send, en_recv, en_s, en_r)
    sent_all(rs_send, rs_recv, rs_s, rs_r)
    sent_all(ag_send, ag_recv, ag_s, ag_r, same=True)
    for j in range(4):
        @pl.when(valid[j])
        def _():
            ghost(j).wait_send()
            ghost_sum(j).wait_send()

        @pl.when(jnp.logical_and(valid[j], up))
        def _():
            low_ghost(j).wait_send()

    @pl.when(up)
    def _():
        low_copy.wait_send()


def shards(layers, planes, *args):
    velocity, adjoint, corners, shared, stretch, shear_part, thickness, rate_factor, retention, weight = args
    per = OWN_ROWS // layers
    elems = corners.shape[1]
    gathered = -(-(2 * per + 4) // 8) * 8
    f32, bf16 = jnp.float32, jnp.bfloat16
    vmem, dma = pltpu.VMEM, pltpu.SemaphoreType.DMA
    out = pl.pallas_call(
        functools.partial(kernel, layers, planes),
        out_shape=jax.ShapeDtypeStruct((32, 128), f32),
        in_specs=[pl.BlockSpec(memory_space=pl.ANY)] * 10,
        out_specs=pl.BlockSpec(memory_space=pltpu.VMEM),
        scratch_shapes=[vmem(a.shape, a.dtype) for a in args]
        + [
            vmem((ALL_ROWS * 32, WIDE), bf16), vmem((80, WIDE), bf16),
            vmem((64, WIDE), bf16), vmem((64, WIDE), bf16),
            vmem((4, 32, 128), bf16), vmem((4, 32, 128), bf16),
            vmem((4, 16, 128), bf16), vmem((4, 16, 128), bf16),
            vmem((8, elems), f32), vmem((8, elems), f32),
            vmem((layers, 2 * per, WIDE), f32), vmem((layers, 2 * per, WIDE), f32),
            vmem((layers, per, WIDE), f32), vmem((layers, per, WIDE), f32),
            vmem((1, elems), f32), vmem((1, elems), f32), vmem((WIDE, 48), f32),
            vmem((layers, 2 * per, 128), f32), vmem((layers, 2 * per, 128), f32),
            vmem((4, 1, 128), f32), vmem((4, 1, 128), f32),
            vmem((gathered, 128), f32), vmem((layers, gathered, 128), f32),
            dma((10,)), dma, dma, dma((4,)), dma((4,)), dma((4,)), dma((4,)),
        ]
        + [dma((layers,)), dma((layers,)), dma((layers,)), dma((layers,)), dma((layers,)), dma((layers,)), dma((4,)), dma((4,)), dma((layers,)), dma((layers,))],
        compiler_params=pltpu.CompilerParams(collective_id=0, has_side_effects=True, vmem_limit_bytes=40 << 20),
        name="ice_gradient",
    )(*args)
    return out.reshape(4096)


def solution(mesh):
    return jax.shard_map(
        functools.partial(shards, mesh.shape["layer"], mesh.shape["plane"]),
        mesh=mesh,
        in_specs=(
            P(None, "layer", "plane"),
            P(None, "layer", "plane"),
            P(None, "plane"),
            P(None, "plane"),
            P(None, "plane"),
            P(None, "plane"),
            P("layer", "plane"),
            P("layer", "plane"),
            P("layer", "plane"),
            P("layer", "plane"),
        ),
        out_specs=P("plane"),
        check_vma=False,
    )
```

```python
import functools
import math

import jax
import jax.numpy as jnp
from jax import lax
from jax.experimental import pallas as pl
from jax.experimental.pallas import tpu as pltpu
from jax.sharding import PartitionSpec as P

OFFSETS = (-2, -1, 1, 2)
STRAIN_EPS = 0.01
GAUSS = 1.0 / math.sqrt(3.0)
MESH = pl.DeviceIdType.MESH
WIDE = 256
OWN_ROWS = 16
ALL_ROWS = 18
GATHER_BLOCK = 2048
MAIN_BLOCK = 1024
SCATTER_BLOCK = 1024


def iota(shape, axis):
    return lax.broadcasted_iota(jnp.int32, shape, axis)


def one_hot(low, width):
    return (iota((width, low.shape[1]), 0) == low).astype(jnp.float32).astype(jnp.bfloat16)


def pick(row, size, table, count):
    out = table[0:size]
    for i in range(1, count):
        out = jnp.where(row == i, table[i * size : (i + 1) * size], out)
    return out


def corner_modes(v):
    p, q, r, s = v[1] - v[0], v[2] - v[3], v[0] + v[1], v[2] + v[3]
    return r + s, p + q, s - r, q - p


def element_terms(upper, lowest, stretch, shear, thick, rate):
    n = thick.shape[1]
    last = iota((8, n), 0) == 7
    top, end = corner_modes(upper), corner_modes(lowest)
    derived = []
    for comp in range(4):
        half, diff = [], []
        for m in range(4):
            t = top[m][comp * 8 : (comp + 1) * 8]
            b = jnp.where(last, pltpu.roll(end[m], 7 - comp, 0), pltpu.roll(t, 7, 0))
            d = t - b
            diff.append(d)
            if m:
                mean = t + b
                gd = GAUSS * d
                half.append((mean - gd, mean + gd))
        mx, my, mxy = half
        xi, eta = [], []
        for z in range(2):
            t = GAUSS * mxy[z]
            xi.append((mx[z] - t, mx[z] + t))
            eta.append((my[z] - t, my[z] + t))
        d0, dx, dy, dxy = diff
        gx, gy, gxy = GAUSS * dx, GAUSS * dy, (GAUSS * GAUSS) * dxy
        a0, a1, b0, b1 = d0 - gx, d0 + gx, gy - gxy, gy + gxy
        derived.append((xi, eta, ((a0 - b0, a0 + b0), (a1 - b1, a1 + b1))))
    s0, s1 = 0.125 * stretch[0:1], 0.125 * stretch[1:2]
    h0, h1 = 0.125 * shear[0:1], 0.125 * shear[1:2]
    inv = 0.125 / thick

    def strains(first, second):
        axi, aeta, az = derived[first]
        bxi, beta, bz = derived[second]
        two = range(2)
        return (
            [[s0 * axi[z][e] for e in two] for z in two],
            [[h0 * aeta[z][x] for x in two] for z in two],
            [[h1 * bxi[z][e] for e in two] for z in two],
            [[s1 * beta[z][x] for x in two] for z in two],
            [[h1 * axi[z][e] + s0 * bxi[z][e] for e in two] for z in two],
            [[s1 * aeta[z][x] + h0 * beta[z][x] for x in two] for z in two],
            [[inv * az[x][e] for e in two] for x in two],
            [[inv * bz[x][e] for e in two] for x in two],
        )

    f, g = strains(0, 1), strains(2, 3)
    total = None
    for x in range(2):
        for e in range(2):
            fxz, fyz, gxz, gyz = f[6][x][e], f[7][x][e], g[6][x][e], g[7][x][e]
            own_z = fxz * fxz + fyz * fyz + STRAIN_EPS
            cross_z = fxz * gxz + fyz * gyz
            for z in range(2):
                fxx, fyy = f[0][z][e] + f[1][z][x], f[2][z][e] + f[3][z][x]
                fxy = 0.5 * (f[4][z][e] + f[5][z][x])
                gxx, gyy = g[0][z][e] + g[1][z][x], g[2][z][e] + g[3][z][x]
                gxy = 0.5 * (g[4][z][e] + g[5][z][x])
                a, b = fxx + 0.5 * fyy, fyy + 0.5 * fxx
                effective = fxx * a + fyy * b + fxy * fxy + own_z
                cross = gxx * a + gyy * b + fxy * gxy + cross_z
                term = jnp.exp2((-1.0 / 3.0) * jnp.log2(effective)) * cross
                total = term if total is None else total + term
    det = stretch[0:1] * stretch[1:2] - shear[0:1] * shear[1:2]
    return (rate * thick) * (total / det)


def recurrence(keep, wei):
    sub = iota(keep.shape, 0)
    factor, offset = keep, (1.0 - keep) * wei
    for d in (1, 2, 4):
        before_f = jnp.where(sub >= d, pltpu.roll(factor, d, 0), 1.0)
        before_o = jnp.where(sub >= d, pltpu.roll(offset, d, 0), 0.0)
        offset = factor * before_o + offset
        factor = factor * before_f
    return factor, offset


def split_bf16(x):
    high = x.astype(jnp.bfloat16).astype(jnp.float32)
    return high, x - high


def kernel(
    layers,
    planes,
    vel_hbm, adj_hbm, cor_hbm, sha_hbm, str_hbm, she_hbm, thi_hbm, rat_hbm, ret_hbm, wei_hbm,
    out,
    vel, adj, corners, shared, stretch, shear, thick, rate, ret, wei,
    table, late, hot, held, low_send, low_own, gsend, grecv, lsend, lrecv,
    fac, off, sc_send, sc_recv, en_send, en_recv,
    abuf, bbuf, acc,
    rs_send, rs_recv, gh_send, gh_recv, ag_send, ag_recv,
    in_sem, low_s, low_r, g_s, g_r, l_s, l_r, sc_s, sc_r, en_s, en_r, rs_s, rs_r, gh_s, gh_r, ag_s, ag_r,
):
    g, p = lax.axis_index("layer"), lax.axis_index("plane")
    per = OWN_ROWS // layers
    f32, bf16 = jnp.float32, jnp.bfloat16

    hbm = (vel_hbm, adj_hbm, sha_hbm, ret_hbm, wei_hbm, cor_hbm, str_hbm, she_hbm, thi_hbm, rat_hbm)
    own = (vel, adj, shared, ret, wei, corners, stretch, shear, thick, rate)
    loads = [pltpu.make_async_copy(a, b, in_sem.at[i]) for i, (a, b) in enumerate(zip(hbm, own))]
    for load in loads:
        load.start()

    valid = [jnp.logical_and(p + o >= 0, p + o < planes) for o in OFFSETS]
    up, down = g > 0, g < layers - 1

    for d in range(4):
        @pl.when(jnp.logical_not(valid[d]))
        def _():
            grecv[d] = jnp.zeros(grecv.shape[1:], bf16)
            lrecv[d] = jnp.zeros(lrecv.shape[1:], bf16)
            gh_recv[d] = jnp.zeros(gh_recv.shape[1:], f32)

    @pl.when(jnp.logical_not(down))
    def _():
        low_own[...] = jnp.zeros(low_own.shape, bf16)
        lrecv[...] = jnp.zeros(lrecv.shape, bf16)

    barrier = pltpu.get_barrier_semaphore()

    def greet(layer, plane):
        pl.semaphore_signal(barrier, inc=1, device_id=(layer, plane), device_id_type=MESH)

    def greet_layer(r, _):
        greet(lax.rem(g + r, layers), p)
        return 0

    lax.fori_loop(1, layers, greet_layer, 0)
    expected = layers - 1
    for d, o in enumerate(OFFSETS):
        @pl.when(valid[d])
        def _():
            greet(g, p + o)

        @pl.when(jnp.logical_and(valid[d], up))
        def _():
            greet(g - 1, p + o)

        @pl.when(jnp.logical_and(valid[d], down))
        def _():
            greet(g + 1, p + o)

        expected = expected + valid[d].astype(jnp.int32) * (1 + up.astype(jnp.int32) + down.astype(jnp.int32))

    loads[0].wait()
    loads[1].wait()
    for i in range(OWN_ROWS):
        at = slice(i * WIDE, (i + 1) * WIDE)
        table[i * 32 : (i + 1) * 32] = jnp.concatenate(
            [vel[0, :, at], vel[1, :, at], adj[0, :, at], adj[1, :, at]], axis=0
        )
    row8 = iota((8, WIDE), 0)
    pieces = []
    for i in range(0, OWN_ROWS, 2):
        piece = jnp.zeros((8, WIDE), f32)
        for half in range(2):
            for comp in range(4):
                level = (vel, adj)[comp // 2][comp % 2, :, (i + half) * WIDE : (i + half + 1) * WIDE].astype(f32)
                piece = jnp.where(row8 == half * 4 + comp, level[0:1], piece)
        pieces.append(piece)
    low_send[...] = jnp.concatenate(pieces, axis=0).astype(bf16)
    loads[2].wait()
    row16 = iota((16, 128), 0)
    for j in range(4):
        ids = shared[j : j + 1, :]
        sent = jnp.dot(table[...], one_hot(ids & (WIDE - 1), WIDE), preferred_element_type=f32)
        sent = pick(ids >> 8, 32, sent, OWN_ROWS)
        gsend[j] = sent.astype(bf16)
        tops = jnp.zeros((16, 128), f32)
        for comp in range(4):
            tops = jnp.where(row16 == comp, sent[comp * 8 : comp * 8 + 1], tops)
        lsend[j] = tops.astype(bf16)
    loads[3].wait()
    loads[4].wait()
    for i in range(8):
        at = slice(i * 512, (i + 1) * 512)
        factor, offset = recurrence(ret[:, at], wei[:, at])
        fac[:, at] = factor
        off[:, at] = offset
    for i in range(layers):
        for k in range(per):
            at = slice((i * per + k) * WIDE, (i * per + k + 1) * WIDE)
            sc_send[i, k : k + 1, :] = fac[7:8, at]
            sc_send[i, per + k : per + k + 1, :] = off[7:8, at]

    pl.semaphore_wait(barrier, expected)

    def remote(src, dst, s, r, layer, plane):
        return pltpu.make_async_remote_copy(
            src_ref=src, dst_ref=dst, send_sem=s, recv_sem=r, device_id=(layer, plane), device_id_type=MESH
        )

    def to_all(send, recv, s, r, same=False):
        def copy(i):
            return remote(send if same else send.at[i], recv.at[g], s.at[i], r.at[g], i, p)

        def start(k, _):
            copy(lax.rem(g + k, layers)).start()
            return 0

        lax.fori_loop(1, layers, start, 0)

    def from_all(send, recv, s, r, same=False):
        def wait(k, _):
            i = lax.rem(g + k, layers)
            remote(send if same else send.at[i], recv.at[i], s.at[i], r.at[i], i, p).wait_recv()
            return 0

        lax.fori_loop(1, layers, wait, 0)

    def sent_all(send, recv, s, r, same=False):
        def wait(k, _):
            i = lax.rem(g + k, layers)
            remote(send if same else send.at[i], recv.at[i], s.at[i], r.at[i], i, p).wait_send()
            return 0

        lax.fori_loop(1, layers, wait, 0)

    def ghost(j):
        return remote(gsend.at[j], grecv.at[3 - j], g_s.at[j], g_r.at[3 - j], g, p + OFFSETS[j])

    def low_ghost(j):
        return remote(lsend.at[j], lrecv.at[3 - j], l_s.at[j], l_r.at[3 - j], g - 1, p + OFFSETS[j])

    low_copy = remote(low_send, low_own, low_s, low_r, g - 1, p)

    to_all(sc_send, sc_recv, sc_s, sc_r)
    for j in range(4):
        @pl.when(valid[j])
        def _():
            ghost(j).start()

        @pl.when(jnp.logical_and(valid[j], up))
        def _():
            low_ghost(j).start()

    @pl.when(up)
    def _():
        low_copy.start()

    def gather_block(b, _):
        c = lax.rem(b, 4)
        at = pl.ds(pl.multiple_of(b // 4 * GATHER_BLOCK, GATHER_BLOCK), GATHER_BLOCK)
        ids = corners[pl.ds(c, 1), at]
        spot = one_hot(ids & (WIDE - 1), WIDE)
        hot[c, :, at] = spot
        held[c, :, at] = pick(ids >> 8, 32, jnp.dot(table[...], spot, preferred_element_type=f32), OWN_ROWS)
        return 0

    gathers = corners.shape[1] // GATHER_BLOCK * 4
    loads[5].wait()
    lax.fori_loop(0, gathers // 2, gather_block, 0)

    sc_recv[g] = sc_send[g]
    from_all(sc_send, sc_recv, sc_s, sc_r)
    running = jnp.zeros((per, WIDE), f32)
    for i in range(layers):
        en_send[i] = running
        running = sc_recv[i, 0:per, :] * running + sc_recv[i, per : 2 * per, :]
    to_all(en_send, en_recv, en_s, en_r)
    en_recv[g] = en_send[g]

    lax.fori_loop(gathers // 2, gathers, gather_block, 0)
    for load in loads[6:]:
        load.wait()

    for j in range(4):
        @pl.when(valid[j])
        def _():
            remote(gsend.at[j], grecv.at[j], g_s.at[j], g_r.at[j], g, p + OFFSETS[j]).wait_recv()

        @pl.when(jnp.logical_and(valid[j], down))
        def _():
            remote(lsend.at[j], lrecv.at[j], l_s.at[j], l_r.at[j], g, p + OFFSETS[j]).wait_recv()

    @pl.when(down)
    def _():
        low_copy.wait_recv()

    for i in range(2):
        late[i * 32 : (i + 1) * 32] = jnp.concatenate([grecv[2 * i], grecv[2 * i + 1]], axis=1)
    late[64:128] = low_own[...]
    first = jnp.concatenate([lrecv[0], lrecv[1]], axis=1).astype(f32)[0:8]
    second = jnp.concatenate([lrecv[2], lrecv[3]], axis=1).astype(f32)[0:8]
    ghosts8 = first + pltpu.roll(second, 4, 0)
    late[128:144] = jnp.concatenate([ghosts8, jnp.zeros((8, WIDE), f32)], axis=0).astype(bf16)

    def main_block(b, _):
        at = pl.ds(pl.multiple_of(b * MAIN_BLOCK, MAIN_BLOCK), MAIN_BLOCK)
        upper, lowest = [], []
        for c in range(4):
            row = corners[c : c + 1, at] >> 8
            found = jnp.dot(late[...], hot[c, :, at], preferred_element_type=f32)
            upper.append(jnp.where(row == 17, found[32:64], jnp.where(row == 16, found[0:32], held[c, :, at])))
            both = pick(row >> 1, 8, found[64:136], ALL_ROWS // 2)
            lowest.append(jnp.where((row & 1) == 1, pltpu.roll(both, 4, 0), both))
        term = element_terms(upper, lowest, stretch[:, at], shear[:, at], thick[:, at], rate[:, at])
        abuf[:, at] = jnp.sum(fac[:, at] * term, axis=0, keepdims=True)
        bbuf[:, at] = jnp.sum(off[:, at] * term, axis=0, keepdims=True)
        return 0

    lax.fori_loop(0, corners.shape[1] // MAIN_BLOCK, main_block, 0)

    from_all(en_send, en_recv, en_s, en_r)
    for i in range(layers):
        for k in range(per):
            at = slice((i * per + k) * WIDE, (i * per + k + 1) * WIDE)
            abuf[:, at] = 0.25 * (abuf[:, at] * en_recv[i, k : k + 1, :] + bbuf[:, at])

    acc[...] = jnp.zeros(acc.shape, f32)

    def scatter_block(b, _):
        at = pl.ds(pl.multiple_of(b * SCATTER_BLOCK, SCATTER_BLOCK), SCATTER_BLOCK)
        row48 = iota((48, SCATTER_BLOCK), 0)
        high, low = split_bf16(abuf[:, at])
        value = jnp.where(row48 < 24, high, low)
        place = jnp.where(row48 < 24, row48, row48 - 24)
        out48 = None
        for c in range(4):
            ids = corners[c : c + 1, at]
            spread = jnp.where(place == (ids >> 8), value, 0.0).astype(bf16)
            part = lax.dot_general(
                hot[c, :, at], spread, (((1,), (1,)), ((), ())), preferred_element_type=f32
            )
            out48 = part if out48 is None else out48 + part
        acc[...] += out48
        return 0

    lax.fori_loop(0, corners.shape[1] // SCATTER_BLOCK, scatter_block, 0)
    nodes = acc[...].T
    nodes = nodes[0:24] + nodes[24:48]
    for i in range(layers):
        for k in range(per):
            lo = i * per + k
            rs_send[i, 2 * k : 2 * k + 1, :] = nodes[lo : lo + 1, 0:128]
            rs_send[i, 2 * k + 1 : 2 * k + 2, :] = nodes[lo : lo + 1, 128:256]
    for j in range(4):
        gh_send[j] = nodes[OWN_ROWS + j // 2 : OWN_ROWS + j // 2 + 1, (j % 2) * 128 : (j % 2 + 1) * 128]

    def ghost_sum(j):
        return remote(gh_send.at[j], gh_recv.at[3 - j], gh_s.at[j], gh_r.at[3 - j], g, p + OFFSETS[j])

    for j in range(4):
        @pl.when(valid[j])
        def _():
            ghost_sum(j).start()
    to_all(rs_send, rs_recv, rs_s, rs_r)
    rs_recv[g] = rs_send[g]

    hots, spots = [], []
    row64 = iota((64, 128), 0) & 31
    for d in range(4):
        ids = shared[d : d + 1, :]
        hots.append(one_hot(ids & 127, 128))
        spots.append(row64 == (ids >> 7))

    for j in range(4):
        @pl.when(valid[j])
        def _():
            remote(gh_send.at[j], gh_recv.at[j], gh_s.at[j], gh_r.at[j], g, p + OFFSETS[j]).wait_recv()
    from_all(rs_send, rs_recv, rs_s, rs_r)
    total = rs_recv[0]
    for i in range(1, layers):
        total = total + rs_recv[i]
    ag_send[0 : 2 * per] = total
    for d in range(4):
        ag_send[2 * per + d : 2 * per + d + 1] = gh_recv[d]
    spare = ag_send.shape[0] - 2 * per - 4
    if spare:
        ag_send[2 * per + 4 :] = jnp.zeros((spare, 128), f32)
    to_all(ag_send, ag_recv, ag_s, ag_r, same=True)
    ag_recv[g] = ag_send[...]
    from_all(ag_send, ag_recv, ag_s, ag_r, same=True)

    arrived = ag_recv[0]
    for i in range(1, layers):
        arrived = arrived + ag_recv[i]
    result = jnp.concatenate([ag_recv[i, 0 : 2 * per, :] for i in range(layers)], axis=0)
    added = None
    half64 = iota((64, 128), 0) < 32
    for d in range(4):
        high, low = split_bf16(arrived[2 * per + d : 2 * per + d + 1])
        spread = jnp.where(spots[d], jnp.where(half64, high, low), 0.0).astype(bf16)
        part = lax.dot_general(spread, hots[d], (((1,), (1,)), ((), ())), preferred_element_type=f32)
        added = part if added is None else added + part
    out[...] = result + (added[0:32] + added[32:64])

    sent_all(sc_send, sc_recv, sc_s, sc_r)
    sent_all(en_send, en_recv, en_s, en_r)
    sent_all(rs_send, rs_recv, rs_s, rs_r)
    sent_all(ag_send, ag_recv, ag_s, ag_r, same=True)
    for j in range(4):
        @pl.when(valid[j])
        def _():
            ghost(j).wait_send()
            ghost_sum(j).wait_send()

        @pl.when(jnp.logical_and(valid[j], up))
        def _():
            low_ghost(j).wait_send()

    @pl.when(up)
    def _():
        low_copy.wait_send()


def shards(layers, planes, *args):
    velocity, adjoint, corners, shared, stretch, shear_part, thickness, rate_factor, retention, weight = args
    per = OWN_ROWS // layers
    elems = corners.shape[1]
    gathered = -(-(2 * per + 4) // 8) * 8
    f32, bf16 = jnp.float32, jnp.bfloat16
    vmem, dma = pltpu.VMEM, pltpu.SemaphoreType.DMA
    out = pl.pallas_call(
        functools.partial(kernel, layers, planes),
        out_shape=jax.ShapeDtypeStruct((32, 128), f32),
        in_specs=[pl.BlockSpec(memory_space=pltpu.HBM)] * 10,
        out_specs=pl.BlockSpec(memory_space=pltpu.VMEM),
        scratch_shapes=[vmem(a.shape, a.dtype) for a in args]
        + [
            vmem((OWN_ROWS * 32, WIDE), bf16), vmem((144, WIDE), bf16),
            vmem((4, WIDE, elems), bf16), vmem((4, 32, elems), f32),
            vmem((64, WIDE), bf16), vmem((64, WIDE), bf16),
            vmem((4, 32, 128), bf16), vmem((4, 32, 128), bf16),
            vmem((4, 16, 128), bf16), vmem((4, 16, 128), bf16),
            vmem((8, elems), f32), vmem((8, elems), f32),
            vmem((layers, 2 * per, WIDE), f32), vmem((layers, 2 * per, WIDE), f32),
            vmem((layers, per, WIDE), f32), vmem((layers, per, WIDE), f32),
            vmem((1, elems), f32), vmem((1, elems), f32), vmem((WIDE, 48), f32),
            vmem((layers, 2 * per, 128), f32), vmem((layers, 2 * per, 128), f32),
            vmem((4, 1, 128), f32), vmem((4, 1, 128), f32),
            vmem((gathered, 128), f32), vmem((layers, gathered, 128), f32),
            dma((10,)), dma, dma, dma((4,)), dma((4,)), dma((4,)), dma((4,)),
        ]
        + [dma((layers,)), dma((layers,)), dma((layers,)), dma((layers,)), dma((layers,)), dma((layers,)), dma((4,)), dma((4,)), dma((layers,)), dma((layers,))],
        compiler_params=pltpu.CompilerParams(collective_id=0, has_side_effects=True, vmem_limit_bytes=60 << 20),
        name="ice_gradient",
    )(*args)
    return out.reshape(4096)


def solution(mesh):
    return jax.shard_map(
        functools.partial(shards, mesh.shape["layer"], mesh.shape["plane"]),
        mesh=mesh,
        in_specs=(
            P(None, "layer", "plane"),
            P(None, "layer", "plane"),
            P(None, "plane"),
            P(None, "plane"),
            P(None, "plane"),
            P(None, "plane"),
            P("layer", "plane"),
            P("layer", "plane"),
            P("layer", "plane"),
            P("layer", "plane"),
        ),
        out_specs=P("plane"),
        check_vma=False,
    )
```

```python
import functools
import math

import jax
import jax.numpy as jnp
from jax import lax
from jax.experimental import pallas as pl
from jax.experimental.pallas import tpu as pltpu
from jax.sharding import PartitionSpec as P

OFFSETS = (-2, -1, 1, 2)
STRAIN_EPS = 0.01
GAUSS = 1.0 / math.sqrt(3.0)
MESH = pl.DeviceIdType.MESH
WIDE = 256
HALF = 2048
OWN_ROWS = 16
ALL_ROWS = 18
GATHER_BLOCK = 4096
MAIN_BLOCK = 1024
SCATTER_BLOCK = 4096


def far_first(k, count):
    return count // 2 + (k + 1) // 2 * (2 * lax.rem(k, 2) - 1)


def iota(shape, axis):
    return lax.broadcasted_iota(jnp.int32, shape, axis)


def one_hot(low, width):
    return (iota((width, low.shape[1]), 0) == low).astype(jnp.float32).astype(jnp.bfloat16)


def place_of(ids):
    owned = ids < 2 * HALF
    row = jnp.where(owned, (ids >> 7) & 15, ids >> 8)
    spot = jnp.where(owned, (ids & 127) | ((ids >> 4) & 128), ids & 255)
    return row, spot


def owned_row(ref, lead, i):
    return jnp.concatenate([ref[lead, :, i * 128 : (i + 1) * 128], ref[lead, :, HALF + i * 128 : HALF + (i + 1) * 128]], axis=1)


def pick(row, size, table, count):
    out = table[0:size]
    for i in range(1, count):
        out = jnp.where(row == i, table[i * size : (i + 1) * size], out)
    return out


def corner_modes(v):
    p, q, r, s = v[1] - v[0], v[2] - v[3], v[0] + v[1], v[2] + v[3]
    return r + s, p + q, s - r, q - p


def element_terms(upper, lowest, stretch, shear, thick, rate):
    n = thick.shape[1]
    last = iota((8, n), 0) == 7
    top, end = corner_modes(upper), corner_modes(lowest)
    derived = []
    for comp in range(4):
        half, diff = [], []
        for m in range(4):
            t = top[m][comp * 8 : (comp + 1) * 8]
            b = jnp.where(last, pltpu.roll(end[m], 7 - comp, 0), pltpu.roll(t, 7, 0))
            d = t - b
            diff.append(d)
            if m:
                mean = t + b
                gd = GAUSS * d
                half.append((mean - gd, mean + gd))
        mx, my, mxy = half
        xi, eta = [], []
        for z in range(2):
            t = GAUSS * mxy[z]
            xi.append((mx[z] - t, mx[z] + t))
            eta.append((my[z] - t, my[z] + t))
        d0, dx, dy, dxy = diff
        gx, gy, gxy = GAUSS * dx, GAUSS * dy, (GAUSS * GAUSS) * dxy
        a0, a1, b0, b1 = d0 - gx, d0 + gx, gy - gxy, gy + gxy
        derived.append((xi, eta, ((a0 - b0, a0 + b0), (a1 - b1, a1 + b1))))
    s0, s1 = 0.125 * stretch[0:1], 0.125 * stretch[1:2]
    h0, h1 = 0.125 * shear[0:1], 0.125 * shear[1:2]
    inv = 0.125 / thick

    def strains(first, second):
        axi, aeta, az = derived[first]
        bxi, beta, bz = derived[second]
        two = range(2)
        return (
            [[s0 * axi[z][e] for e in two] for z in two],
            [[h0 * aeta[z][x] for x in two] for z in two],
            [[h1 * bxi[z][e] for e in two] for z in two],
            [[s1 * beta[z][x] for x in two] for z in two],
            [[h1 * axi[z][e] + s0 * bxi[z][e] for e in two] for z in two],
            [[s1 * aeta[z][x] + h0 * beta[z][x] for x in two] for z in two],
            [[inv * az[x][e] for e in two] for x in two],
            [[inv * bz[x][e] for e in two] for x in two],
        )

    f, g = strains(0, 1), strains(2, 3)
    total = None
    for x in range(2):
        for e in range(2):
            fxz, fyz, gxz, gyz = f[6][x][e], f[7][x][e], g[6][x][e], g[7][x][e]
            own_z = fxz * fxz + fyz * fyz + STRAIN_EPS
            cross_z = fxz * gxz + fyz * gyz
            for z in range(2):
                fxx, fyy = f[0][z][e] + f[1][z][x], f[2][z][e] + f[3][z][x]
                fxy = 0.5 * (f[4][z][e] + f[5][z][x])
                gxx, gyy = g[0][z][e] + g[1][z][x], g[2][z][e] + g[3][z][x]
                gxy = 0.5 * (g[4][z][e] + g[5][z][x])
                a, b = fxx + 0.5 * fyy, fyy + 0.5 * fxx
                effective = fxx * a + fyy * b + fxy * fxy + own_z
                cross = gxx * a + gyy * b + fxy * gxy + cross_z
                term = jnp.exp2((-1.0 / 3.0) * jnp.log2(effective)) * cross
                total = term if total is None else total + term
    det = stretch[0:1] * stretch[1:2] - shear[0:1] * shear[1:2]
    return (rate * thick) * (total / det)


def recurrence(keep, wei):
    sub = iota(keep.shape, 0)
    factor, offset = keep, (1.0 - keep) * wei
    for d in (1, 2, 4):
        before_f = jnp.where(sub >= d, pltpu.roll(factor, d, 0), 1.0)
        before_o = jnp.where(sub >= d, pltpu.roll(offset, d, 0), 0.0)
        offset = factor * before_o + offset
        factor = factor * before_f
    return factor, offset


def split_bf16(x):
    high = x.astype(jnp.bfloat16).astype(jnp.float32)
    return high, x - high


def kernel(
    layers,
    planes,
    vel_hbm, adj_hbm, cor_hbm, sha_hbm, str_hbm, she_hbm, thi_hbm, rat_hbm, ret_hbm, wei_hbm,
    out,
    vel, adj, corners, shared, stretch, shear, thick, rate, ret, wei,
    table, late, late8, hot, held, rows, low_send, low_own, gsend, grecv, lsend, lrecv,
    fac, off, sc_send, sc_recv, en_send, en_recv,
    abuf, bbuf,
    gh_send, gh_recv, pair_send, pair_recv, all_recv, done,
    in_sem, low_s, low_r, g_s, g_r, l_s, l_r, sc_s, sc_r, en_s, en_r, gh_s, gh_r, pair_s, pair_r, all_s, all_r, last_s, last_r,
):
    g, p = lax.axis_index("layer"), lax.axis_index("plane")
    per = OWN_ROWS // layers
    f32, bf16 = jnp.float32, jnp.bfloat16

    hbm = (vel_hbm, adj_hbm, sha_hbm, ret_hbm, wei_hbm, cor_hbm, str_hbm, she_hbm, thi_hbm, rat_hbm)
    own = (vel, adj, shared, ret, wei, corners, stretch, shear, thick, rate)
    loads = [pltpu.make_async_copy(a, b, in_sem.at[i]) for i, (a, b) in enumerate(zip(hbm, own))]
    for load in loads:
        load.start()

    valid = [jnp.logical_and(p + o >= 0, p + o < planes) for o in OFFSETS]
    up, down = g > 0, g < layers - 1

    for d in range(4):
        @pl.when(jnp.logical_not(valid[d]))
        def _():
            grecv[d] = jnp.zeros(grecv.shape[1:], bf16)
            lrecv[d] = jnp.zeros(lrecv.shape[1:], bf16)
            gh_recv[d] = jnp.zeros(gh_recv.shape[1:], f32)

    @pl.when(jnp.logical_not(down))
    def _():
        low_own[...] = jnp.zeros(low_own.shape, bf16)
        lrecv[...] = jnp.zeros(lrecv.shape, bf16)

    barrier = pltpu.get_barrier_semaphore()

    def greet(layer, plane):
        pl.semaphore_signal(barrier, inc=1, device_id=(layer, plane), device_id_type=MESH)

    def greet_layer(r, _):
        greet(lax.rem(g + r, layers), p)
        return 0

    lax.fori_loop(1, layers, greet_layer, 0)
    expected = layers - 1
    for d, o in enumerate(OFFSETS):
        @pl.when(valid[d])
        def _():
            greet(g, p + o)

        @pl.when(jnp.logical_and(valid[d], up))
        def _():
            greet(g - 1, p + o)

        @pl.when(jnp.logical_and(valid[d], down))
        def _():
            greet(g + 1, p + o)

        expected = expected + valid[d].astype(jnp.int32) * (1 + up.astype(jnp.int32) + down.astype(jnp.int32))

    loads[0].wait()
    loads[1].wait()
    for i in range(OWN_ROWS):
        table[i * 32 : (i + 1) * 32] = jnp.concatenate([owned_row(f, k, i) for f in (vel, adj) for k in range(2)], axis=0)
    row8 = iota((8, WIDE), 0)
    pieces = []
    for i in range(0, OWN_ROWS, 2):
        piece = jnp.zeros((8, WIDE), f32)
        for half in range(2):
            for comp in range(4):
                level = owned_row((vel, adj)[comp // 2], comp % 2, i + half).astype(f32)
                piece = jnp.where(row8 == half * 4 + comp, level[0:1], piece)
        pieces.append(piece)
    low_send[...] = jnp.concatenate(pieces, axis=0).astype(bf16)
    loads[2].wait()
    row16 = iota((16, 128), 0)
    for j in range(4):
        ids = shared[j : j + 1, :]
        row, spot = place_of(ids)
        sent = jnp.dot(table[...], one_hot(spot, WIDE), preferred_element_type=f32)
        sent = pick(row, 32, sent, OWN_ROWS)
        gsend[j] = sent.astype(bf16)
        tops = jnp.zeros((16, 128), f32)
        for comp in range(4):
            tops = jnp.where(row16 == comp, sent[comp * 8 : comp * 8 + 1], tops)
        lsend[j] = tops.astype(bf16)
    loads[3].wait()
    loads[4].wait()
    for i in range(8):
        at = slice(i * 512, (i + 1) * 512)
        factor, offset = recurrence(ret[:, at], wei[:, at])
        fac[:, at] = factor
        off[:, at] = offset
    for i in range(layers):
        for k in range(per):
            at = slice((i * per + k) * WIDE, (i * per + k + 1) * WIDE)
            sc_send[i, k : k + 1, :] = fac[7:8, at]
            sc_send[i, per + k : per + k + 1, :] = off[7:8, at]

    pl.semaphore_wait(barrier, expected)

    def remote(src, dst, s, r, layer, plane):
        return pltpu.make_async_remote_copy(
            src_ref=src, dst_ref=dst, send_sem=s, recv_sem=r, device_id=(layer, plane), device_id_type=MESH
        )

    def to_all(send, recv, s, r):
        def copy(i):
            return remote(send.at[i], recv.at[g], s.at[i], r.at[g], i, p)

        def start(k, _):
            copy(lax.rem(g + far_first(k, layers), layers)).start()
            return 0

        lax.fori_loop(0, layers - 1, start, 0)

    def from_all(send, recv, s, r):
        def wait(k, _):
            i = lax.rem(g + k, layers)
            remote(send.at[i], recv.at[i], s.at[i], r.at[i], i, p).wait_recv()
            return 0

        lax.fori_loop(1, layers, wait, 0)

    def sent_all(send, recv, s, r):
        def wait(k, _):
            i = lax.rem(g + k, layers)
            remote(send.at[i], recv.at[i], s.at[i], r.at[i], i, p).wait_send()
            return 0

        lax.fori_loop(1, layers, wait, 0)

    def ghost(j):
        return remote(gsend.at[j], grecv.at[3 - j], g_s.at[j], g_r.at[3 - j], g, p + OFFSETS[j])

    def low_ghost(j):
        return remote(lsend.at[j], lrecv.at[3 - j], l_s.at[j], l_r.at[3 - j], g - 1, p + OFFSETS[j])

    low_copy = remote(low_send, low_own, low_s, low_r, g - 1, p)

    to_all(sc_send, sc_recv, sc_s, sc_r)
    for j in range(4):
        @pl.when(valid[j])
        def _():
            ghost(j).start()

        @pl.when(jnp.logical_and(valid[j], up))
        def _():
            low_ghost(j).start()

    @pl.when(up)
    def _():
        low_copy.start()

    def gather_block(b, _):
        c = lax.rem(b, 4)
        at = pl.ds(pl.multiple_of(b // 4 * GATHER_BLOCK, GATHER_BLOCK), GATHER_BLOCK)
        row, spot = place_of(corners[pl.ds(c, 1), at])
        spot = one_hot(spot, WIDE)
        rows[pl.ds(c, 1), at] = row
        hot[c, :, at] = spot
        held[c, :, at] = pick(row, 32, jnp.dot(table[...], spot, preferred_element_type=f32), OWN_ROWS)
        return 0

    gathers = corners.shape[1] // GATHER_BLOCK * 4
    loads[5].wait()
    lax.fori_loop(0, gathers, gather_block, 0)

    sc_recv[g] = sc_send[g]
    from_all(sc_send, sc_recv, sc_s, sc_r)
    running = jnp.zeros((per, WIDE), f32)
    for i in range(layers):
        en_send[i] = running
        running = sc_recv[i, 0:per, :] * running + sc_recv[i, per : 2 * per, :]
    to_all(en_send, en_recv, en_s, en_r)
    en_recv[g] = en_send[g]

    for load in loads[6:]:
        load.wait()

    for j in range(4):
        @pl.when(valid[j])
        def _():
            remote(gsend.at[j], grecv.at[j], g_s.at[j], g_r.at[j], g, p + OFFSETS[j]).wait_recv()

        @pl.when(jnp.logical_and(valid[j], down))
        def _():
            remote(lsend.at[j], lrecv.at[j], l_s.at[j], l_r.at[j], g, p + OFFSETS[j]).wait_recv()

    @pl.when(down)
    def _():
        low_copy.wait_recv()

    for i in range(2):
        late[i * 32 : (i + 1) * 32] = jnp.concatenate([grecv[2 * i], grecv[2 * i + 1]], axis=1)
    late8[0:64] = low_own[...]
    first = jnp.concatenate([lrecv[0], lrecv[1]], axis=1).astype(f32)[0:8]
    second = jnp.concatenate([lrecv[2], lrecv[3]], axis=1).astype(f32)[0:8]
    ghosts8 = first + pltpu.roll(second, 4, 0)
    late8[64:80] = jnp.concatenate([ghosts8, jnp.zeros((8, WIDE), f32)], axis=0).astype(bf16)

    def main_block(b, _):
        at = pl.ds(pl.multiple_of(b * MAIN_BLOCK, MAIN_BLOCK), MAIN_BLOCK)
        upper, lowest = [], []
        for c in range(4):
            row = rows[c : c + 1, at]
            if c == 0:
                found = jnp.dot(late[...], hot[c, :, at], preferred_element_type=f32)
                upper.append(jnp.where(row == 17, found[32:64], jnp.where(row == 16, found[0:32], held[c, :, at])))
                found = jnp.dot(late8[...], hot[c, :, at], preferred_element_type=f32)
                both = pick(row >> 1, 8, found, ALL_ROWS // 2)
            else:
                upper.append(held[c, :, at])
                found = jnp.dot(late8[0:64], hot[c, :, at], preferred_element_type=f32)
                both = pick(row >> 1, 8, found, OWN_ROWS // 2)
            lowest.append(jnp.where((row & 1) == 1, pltpu.roll(both, 4, 0), both))
        term = element_terms(upper, lowest, stretch[:, at], shear[:, at], thick[:, at], rate[:, at])
        abuf[:, at] = jnp.sum(fac[:, at] * term, axis=0, keepdims=True)
        bbuf[:, at] = jnp.sum(off[:, at] * term, axis=0, keepdims=True)
        return 0

    lax.fori_loop(0, corners.shape[1] // MAIN_BLOCK, main_block, 0)

    from_all(en_send, en_recv, en_s, en_r)
    for i in range(layers):
        for k in range(per):
            at = slice((i * per + k) * WIDE, (i * per + k + 1) * WIDE)
            abuf[:, at] = 0.25 * (abuf[:, at] * en_recv[i, k : k + 1, :] + bbuf[:, at])

    def scatter(c, count):
        def block(b, total):
            at = slice(b * SCATTER_BLOCK, (b + 1) * SCATTER_BLOCK)
            line = iota((2 * count, SCATTER_BLOCK), 0)
            high, low = split_bf16(abuf[:, at])
            value = jnp.where(line < count, high, low)
            place = jnp.where(line < count, line, line - count)
            spread = jnp.where(place == rows[c : c + 1, at], value, 0.0).astype(bf16)
            return total + lax.dot_general(hot[c, :, at], spread, (((1,), (1,)), ((), ())), preferred_element_type=f32)

        total = block(0, jnp.zeros((WIDE, 2 * count), f32)).T
        return total[0:count] + total[count : 2 * count]

    def ghost_sum(j):
        return remote(gh_send.at[j], gh_recv.at[3 - j], gh_s.at[j], gh_r.at[3 - j], g, p + OFFSETS[j])

    nodes = scatter(0, 24)
    for j in range(4):
        gh_send[j] = nodes[OWN_ROWS + j // 2 : OWN_ROWS + j // 2 + 1, (j % 2) * 128 : (j % 2 + 1) * 128]
    for j in range(4):
        @pl.when(valid[j])
        def _():
            ghost_sum(j).start()
    owned = nodes[0:OWN_ROWS]
    for c in range(1, 4):
        owned = owned + scatter(c, OWN_ROWS)
    owned = jnp.concatenate([owned[:, 0:128], owned[:, 128:256]], axis=0)

    for j in range(4):
        @pl.when(valid[j])
        def _():
            remote(gh_send.at[j], gh_recv.at[j], gh_s.at[j], gh_r.at[j], g, p + OFFSETS[j]).wait_recv()
    row64 = iota((64, 128), 0)
    added = None
    for d in range(4):
        ids = shared[d : d + 1, :]
        high, low = split_bf16(gh_recv[d])
        spread = jnp.where((row64 & 31) == (ids >> 7), jnp.where(row64 < 32, high, low), 0.0).astype(bf16)
        part = lax.dot_general(spread, one_hot(ids & 127, 128), (((1,), (1,)), ((), ())), preferred_element_type=f32)
        added = part if added is None else added + part
    owned = owned + (added[0:32] + added[32:64])

    core, chip, chips = lax.rem(g, 2), g // 2, layers // 2
    mate = g + 1 - 2 * core
    pair_send[0] = owned[0:16]
    pair_send[1] = owned[16:32]
    pair = remote(pair_send.at[1 - core], pair_recv, pair_s, pair_r, mate, p)
    pair.start()
    pair.wait_recv()
    all_recv[chip] = pair_send[core] + pair_recv[...]

    def over_chips(k):
        i = lax.rem(chip + k, chips)
        return remote(all_recv.at[chip], all_recv.at[chip], all_s.at[i], all_r.at[chip], 2 * i + core, p)

    def from_chip(k):
        i = lax.rem(chip + k, chips)
        return remote(all_recv.at[chip], all_recv.at[i], all_s.at[i], all_r.at[i], 2 * i + core, p)

    def start_chip(k, _):
        over_chips(far_first(k, chips)).start()
        return 0

    def wait_chip(k, _):
        from_chip(k).wait_recv()
        return 0

    lax.fori_loop(0, chips - 1, start_chip, 0)
    lax.fori_loop(1, chips, wait_chip, 0)
    total = all_recv[0]
    for i in range(1, chips):
        total = total + all_recv[i]
    done[core] = total
    last = remote(done.at[core], done.at[core], last_s, last_r, mate, p)
    last.start()
    remote(done.at[core], done.at[1 - core], last_s, last_r, mate, p).wait_recv()
    out[0:16] = done[0]
    out[16:32] = done[1]

    def sent_chip(k, _):
        over_chips(k).wait_send()
        return 0

    lax.fori_loop(1, chips, sent_chip, 0)
    pair.wait_send()
    last.wait_send()
    sent_all(sc_send, sc_recv, sc_s, sc_r)
    sent_all(en_send, en_recv, en_s, en_r)
    for j in range(4):
        @pl.when(valid[j])
        def _():
            ghost(j).wait_send()
            ghost_sum(j).wait_send()

        @pl.when(jnp.logical_and(valid[j], up))
        def _():
            low_ghost(j).wait_send()

    @pl.when(up)
    def _():
        low_copy.wait_send()


def shards(layers, planes, *args):
    velocity, adjoint, corners, shared, stretch, shear_part, thickness, rate_factor, retention, weight = args
    per = OWN_ROWS // layers
    elems = corners.shape[1]
    f32, bf16 = jnp.float32, jnp.bfloat16
    vmem, dma = pltpu.VMEM, pltpu.SemaphoreType.DMA
    out = pl.pallas_call(
        functools.partial(kernel, layers, planes),
        out_shape=jax.ShapeDtypeStruct((32, 128), f32),
        in_specs=[pl.BlockSpec(memory_space=pltpu.HBM)] * 10,
        out_specs=pl.BlockSpec(memory_space=pltpu.VMEM),
        scratch_shapes=[vmem(a.shape, a.dtype) for a in args]
        + [
            vmem((OWN_ROWS * 32, WIDE), bf16), vmem((64, WIDE), bf16), vmem((80, WIDE), bf16),
            vmem((4, WIDE, elems), bf16), vmem((4, 32, elems), f32), vmem((4, elems), jnp.int32),
            vmem((64, WIDE), bf16), vmem((64, WIDE), bf16),
            vmem((4, 32, 128), bf16), vmem((4, 32, 128), bf16),
            vmem((4, 16, 128), bf16), vmem((4, 16, 128), bf16),
            vmem((8, elems), f32), vmem((8, elems), f32),
            vmem((layers, 2 * per, WIDE), f32), vmem((layers, 2 * per, WIDE), f32),
            vmem((layers, per, WIDE), f32), vmem((layers, per, WIDE), f32),
            vmem((1, elems), f32), vmem((1, elems), f32),
            vmem((4, 1, 128), f32), vmem((4, 1, 128), f32),
            vmem((2, 16, 128), f32), vmem((16, 128), f32), vmem((layers // 2, 16, 128), f32), vmem((2, 16, 128), f32),
            dma((10,)), dma, dma, dma((4,)), dma((4,)), dma((4,)), dma((4,)),
        ]
        + [dma((layers,)), dma((layers,)), dma((layers,)), dma((layers,)), dma((4,)), dma((4,)), dma, dma]
        + [dma((layers // 2,)), dma((layers // 2,)), dma, dma],
        compiler_params=pltpu.CompilerParams(collective_id=0, has_side_effects=True, vmem_limit_bytes=60 << 20),
        name="ice_gradient",
    )(*args)
    return out.reshape(4096)


def solution(mesh):
    return jax.shard_map(
        functools.partial(shards, mesh.shape["layer"], mesh.shape["plane"]),
        mesh=mesh,
        in_specs=(
            P(None, "layer", "plane"),
            P(None, "layer", "plane"),
            P(None, "plane"),
            P(None, "plane"),
            P(None, "plane"),
            P(None, "plane"),
            P("layer", "plane"),
            P("layer", "plane"),
            P("layer", "plane"),
            P("layer", "plane"),
        ),
        out_specs=P("plane"),
        check_vma=False,
    )
```

```python
import functools
import math

import jax
import jax.numpy as jnp
from jax import lax
from jax.experimental import pallas as pl
from jax.experimental.pallas import tpu as pltpu
from jax.sharding import PartitionSpec as P

OFFSETS = (-2, -1, 1, 2)
STRAIN_EPS = 0.01
GAUSS = 1.0 / math.sqrt(3.0)
MESH = pl.DeviceIdType.MESH
WIDE = 256
HALF = 2048
OWN_ROWS = 16
ALL_ROWS = 18
MAIN_BLOCK = 512
SCATTER_BLOCK = 4096


def far_first(k, count):
    return count // 2 + (k + 1) // 2 * (2 * lax.rem(k, 2) - 1)


def iota(shape, axis):
    return lax.broadcasted_iota(jnp.int32, shape, axis)


def one_hot(low, width):
    return (iota((width, low.shape[1]), 0) == low).astype(jnp.float32).astype(jnp.bfloat16)


def place_of(ids):
    owned = ids < 2 * HALF
    row = jnp.where(owned, (ids >> 7) & 15, ids >> 8)
    spot = jnp.where(owned, (ids & 127) | ((ids >> 4) & 128), ids & 255)
    return row, spot


def owned_row(ref, lead, i):
    return jnp.concatenate([ref[lead, :, i * 128 : (i + 1) * 128], ref[lead, :, HALF + i * 128 : HALF + (i + 1) * 128]], axis=1)


def pick(row, size, table, count):
    out = table[0:size]
    for i in range(1, count):
        out = jnp.where(row == i, table[i * size : (i + 1) * size], out)
    return out


def corner_modes(v):
    p, q, r, s = v[1] - v[0], v[2] - v[3], v[0] + v[1], v[2] + v[3]
    return r + s, p + q, s - r, q - p


def element_terms(upper, lowest, stretch, shear, thick, rate):
    n = thick.shape[1]
    last = iota((8, n), 0) == 7
    top, end = corner_modes(upper), corner_modes(lowest)
    derived = []
    for comp in range(4):
        half, diff = [], []
        for m in range(4):
            t = top[m][comp * 8 : (comp + 1) * 8]
            b = jnp.where(last, pltpu.roll(end[m], 7 - comp, 0), pltpu.roll(t, 7, 0))
            d = t - b
            diff.append(d)
            if m:
                mean = t + b
                gd = GAUSS * d
                half.append((mean - gd, mean + gd))
        mx, my, mxy = half
        xi, eta = [], []
        for z in range(2):
            t = GAUSS * mxy[z]
            xi.append((mx[z] - t, mx[z] + t))
            eta.append((my[z] - t, my[z] + t))
        d0, dx, dy, dxy = diff
        gx, gy, gxy = GAUSS * dx, GAUSS * dy, (GAUSS * GAUSS) * dxy
        a0, a1, b0, b1 = d0 - gx, d0 + gx, gy - gxy, gy + gxy
        derived.append((xi, eta, ((a0 - b0, a0 + b0), (a1 - b1, a1 + b1))))
    s0, s1 = 0.125 * stretch[0:1], 0.125 * stretch[1:2]
    h0, h1 = 0.125 * shear[0:1], 0.125 * shear[1:2]
    inv = 0.125 / thick

    def strains(first, second):
        axi, aeta, az = derived[first]
        bxi, beta, bz = derived[second]
        two = range(2)
        return (
            [[s0 * axi[z][e] for e in two] for z in two],
            [[h0 * aeta[z][x] for x in two] for z in two],
            [[h1 * bxi[z][e] for e in two] for z in two],
            [[s1 * beta[z][x] for x in two] for z in two],
            [[h1 * axi[z][e] + s0 * bxi[z][e] for e in two] for z in two],
            [[s1 * aeta[z][x] + h0 * beta[z][x] for x in two] for z in two],
            [[inv * az[x][e] for e in two] for x in two],
            [[inv * bz[x][e] for e in two] for x in two],
        )

    f, g = strains(0, 1), strains(2, 3)
    total = None
    for x in range(2):
        for e in range(2):
            fxz, fyz, gxz, gyz = f[6][x][e], f[7][x][e], g[6][x][e], g[7][x][e]
            own_z = fxz * fxz + fyz * fyz + STRAIN_EPS
            cross_z = fxz * gxz + fyz * gyz
            for z in range(2):
                fxx, fyy = f[0][z][e] + f[1][z][x], f[2][z][e] + f[3][z][x]
                fxy = 0.5 * (f[4][z][e] + f[5][z][x])
                gxx, gyy = g[0][z][e] + g[1][z][x], g[2][z][e] + g[3][z][x]
                gxy = 0.5 * (g[4][z][e] + g[5][z][x])
                a, b = fxx + 0.5 * fyy, fyy + 0.5 * fxx
                effective = fxx * a + fyy * b + fxy * fxy + own_z
                cross = gxx * a + gyy * b + fxy * gxy + cross_z
                term = jnp.exp2((-1.0 / 3.0) * jnp.log2(effective)) * cross
                total = term if total is None else total + term
    det = stretch[0:1] * stretch[1:2] - shear[0:1] * shear[1:2]
    return (rate * thick) * (total / det)


def recurrence(keep, wei):
    sub = iota(keep.shape, 0)
    factor, offset = keep, (1.0 - keep) * wei
    for d in (1, 2, 4):
        before_f = jnp.where(sub >= d, pltpu.roll(factor, d, 0), 1.0)
        before_o = jnp.where(sub >= d, pltpu.roll(offset, d, 0), 0.0)
        offset = factor * before_o + offset
        factor = factor * before_f
    return factor, offset


def split_bf16(x):
    high = x.astype(jnp.bfloat16).astype(jnp.float32)
    return high, x - high


def kernel(
    layers,
    planes,
    vel_hbm, adj_hbm, cor_hbm, sha_hbm, str_hbm, she_hbm, thi_hbm, rat_hbm, ret_hbm, wei_hbm,
    out,
    vel, adj, corners, shared, stretch, shear, thick, rate, ret, wei,
    table, late, late8, hot, held, rows, low0, top_send, top_recv, low_send, low_own, gsend, grecv, lsend, lrecv,
    fac, off, sc_send, sc_recv, en_send, en_recv,
    abuf, bbuf,
    gh_send, gh_recv, pair_send, pair_recv, all_recv, done,
    in_sem, low_s, low_r, top_s, top_r, g_s, g_r, l_s, l_r, sc_s, sc_r, en_s, en_r, gh_s, gh_r, pair_s, pair_r, all_s, all_r, last_s, last_r,
):
    g, p = lax.axis_index("layer"), lax.axis_index("plane")
    per = OWN_ROWS // layers
    f32, bf16 = jnp.float32, jnp.bfloat16

    hbm = (vel_hbm, adj_hbm, sha_hbm, ret_hbm, wei_hbm, cor_hbm, str_hbm, she_hbm, thi_hbm, rat_hbm)
    own = (vel, adj, shared, ret, wei, corners, stretch, shear, thick, rate)
    loads = [pltpu.make_async_copy(a, b, in_sem.at[i]) for i, (a, b) in enumerate(zip(hbm, own))]
    for load in loads:
        load.start()

    valid = [jnp.logical_and(p + o >= 0, p + o < planes) for o in OFFSETS]
    up, down = g > 0, g < layers - 1

    for d in range(4):
        @pl.when(jnp.logical_not(valid[d]))
        def _():
            grecv[d] = jnp.zeros(grecv.shape[1:], bf16)
            lrecv[d] = jnp.zeros(lrecv.shape[1:], bf16)
            gh_recv[d] = jnp.zeros(gh_recv.shape[1:], f32)

    @pl.when(jnp.logical_not(down))
    def _():
        low_own[...] = jnp.zeros(low_own.shape, bf16)
        lrecv[...] = jnp.zeros(lrecv.shape, bf16)
        top_recv[...] = jnp.zeros(top_recv.shape, bf16)

    barrier = pltpu.get_barrier_semaphore()

    def greet(layer, plane):
        pl.semaphore_signal(barrier, inc=1, device_id=(layer, plane), device_id_type=MESH)

    def greet_layer(r, _):
        greet(lax.rem(g + r, layers), p)
        return 0

    lax.fori_loop(1, layers, greet_layer, 0)
    expected = layers - 1
    for d, o in enumerate(OFFSETS):
        @pl.when(valid[d])
        def _():
            greet(g, p + o)

        @pl.when(jnp.logical_and(valid[d], up))
        def _():
            greet(g - 1, p + o)

        @pl.when(jnp.logical_and(valid[d], down))
        def _():
            greet(g + 1, p + o)

        expected = expected + valid[d].astype(jnp.int32) * (1 + up.astype(jnp.int32) + down.astype(jnp.int32))

    loads[0].wait()
    loads[1].wait()
    for i in range(OWN_ROWS):
        table[i * 32 : (i + 1) * 32] = jnp.concatenate([owned_row(f, k, i) for f in (vel, adj) for k in range(2)], axis=0)
    row8 = iota((8, WIDE), 0)
    pieces = []
    for i in range(0, OWN_ROWS, 2):
        piece = jnp.zeros((8, WIDE), f32)
        for half in range(2):
            for comp in range(4):
                level = owned_row((vel, adj)[comp // 2], comp % 2, i + half).astype(f32)
                piece = jnp.where(row8 == half * 4 + comp, level[0:1], piece)
        pieces.append(piece)
    low_send[...] = jnp.concatenate(pieces, axis=0).astype(bf16)
    loads[2].wait()
    row16 = iota((16, 128), 0)
    for j in range(4):
        ids = shared[j : j + 1, :]
        row, spot = place_of(ids)
        sent = jnp.dot(table[...], one_hot(spot, WIDE), preferred_element_type=f32)
        sent = pick(row, 32, sent, OWN_ROWS)
        gsend[j] = sent.astype(bf16)
        tops = jnp.zeros((16, 128), f32)
        for comp in range(4):
            tops = jnp.where(row16 == comp, sent[comp * 8 : comp * 8 + 1], tops)
        lsend[j] = tops.astype(bf16)
    loads[3].wait()
    loads[4].wait()
    for i in range(8):
        at = slice(i * 512, (i + 1) * 512)
        factor, offset = recurrence(ret[:, at], wei[:, at])
        fac[:, at] = factor
        off[:, at] = offset
    for i in range(layers):
        for k in range(per):
            at = slice((i * per + k) * WIDE, (i * per + k + 1) * WIDE)
            sc_send[i, k : k + 1, :] = fac[7:8, at]
            sc_send[i, per + k : per + k + 1, :] = off[7:8, at]

    pl.semaphore_wait(barrier, expected)

    def remote(src, dst, s, r, layer, plane):
        return pltpu.make_async_remote_copy(
            src_ref=src, dst_ref=dst, send_sem=s, recv_sem=r, device_id=(layer, plane), device_id_type=MESH
        )

    def to_all(send, recv, s, r):
        def copy(i):
            return remote(send.at[i], recv.at[g], s.at[i], r.at[g], i, p)

        def start(k, _):
            copy(lax.rem(g + far_first(k, layers), layers)).start()
            return 0

        lax.fori_loop(0, layers - 1, start, 0)

    def from_all(send, recv, s, r):
        def wait(k, _):
            i = lax.rem(g + k, layers)
            remote(send.at[i], recv.at[i], s.at[i], r.at[i], i, p).wait_recv()
            return 0

        lax.fori_loop(1, layers, wait, 0)

    def sent_all(send, recv, s, r):
        def wait(k, _):
            i = lax.rem(g + k, layers)
            remote(send.at[i], recv.at[i], s.at[i], r.at[i], i, p).wait_send()
            return 0

        lax.fori_loop(1, layers, wait, 0)

    def ghost(j):
        return remote(gsend.at[j], grecv.at[3 - j], g_s.at[j], g_r.at[3 - j], g, p + OFFSETS[j])

    def low_ghost(j):
        return remote(lsend.at[j], lrecv.at[3 - j], l_s.at[j], l_r.at[3 - j], g - 1, p + OFFSETS[j])

    low_copy = remote(low_send, low_own, low_s, low_r, g - 1, p)

    to_all(sc_send, sc_recv, sc_s, sc_r)

    for j in range(4):
        @pl.when(valid[j])
        def _():
            ghost(j).start()

        @pl.when(jnp.logical_and(valid[j], up))
        def _():
            low_ghost(j).start()

    @pl.when(up)
    def _():
        low_copy.start()

    def top_copy(i):
        return remote(top_send.at[i], top_recv.at[i], top_s.at[i], top_r.at[i], g - 1, p)

    def enter():
        sc_recv[g] = sc_send[g]
        from_all(sc_send, sc_recv, sc_s, sc_r)
        running = jnp.zeros((per, WIDE), f32)
        for i in range(layers):
            en_send[i] = running
            running = sc_recv[i, 0:per, :] * running + sc_recv[i, per : 2 * per, :]
        to_all(en_send, en_recv, en_s, en_r)
        en_recv[g] = en_send[g]

    def gather(b, _):
        @pl.when(b == 3)
        def _():
            enter()

        c = lax.rem(b + 1, 4)
        row, spot = place_of(corners[pl.ds(c, 1), :])
        spot = one_hot(spot, WIDE)
        rows[pl.ds(c, 1), :] = row
        hot[c] = spot
        found = pick(row, 32, jnp.dot(table[...], spot, preferred_element_type=f32), OWN_ROWS)
        held[c] = found

        @pl.when(jnp.logical_and(b < 3, up))
        def _():
            top_send[b] = jnp.concatenate([found[8 * k : 8 * k + 1] for k in range(4)], axis=0).astype(bf16)
            top_copy(b).start()

        return 0

    loads[5].wait()
    lax.fori_loop(0, 4, gather, 0)

    for load in loads[6:]:
        load.wait()

    for j in range(4):
        @pl.when(valid[j])
        def _():
            remote(gsend.at[j], grecv.at[j], g_s.at[j], g_r.at[j], g, p + OFFSETS[j]).wait_recv()

        @pl.when(jnp.logical_and(valid[j], down))
        def _():
            remote(lsend.at[j], lrecv.at[j], l_s.at[j], l_r.at[j], g, p + OFFSETS[j]).wait_recv()

    @pl.when(down)
    def _():
        low_copy.wait_recv()

    for i in range(2):
        late[i * 32 : (i + 1) * 32] = jnp.concatenate([grecv[2 * i], grecv[2 * i + 1]], axis=1)
    late8[0:64] = low_own[...]
    first = jnp.concatenate([lrecv[0], lrecv[1]], axis=1).astype(f32)[0:8]
    second = jnp.concatenate([lrecv[2], lrecv[3]], axis=1).astype(f32)[0:8]
    ghosts8 = first + pltpu.roll(second, 4, 0)
    late8[64:80] = jnp.concatenate([ghosts8, jnp.zeros((8, WIDE), f32)], axis=0).astype(bf16)

    row = rows[0:1, :]
    found = jnp.dot(late[...], hot[0], preferred_element_type=f32)
    held[0] = jnp.where(row == 17, found[32:64], jnp.where(row == 16, found[0:32], held[0]))
    both = pick(row >> 1, 8, jnp.dot(late8[...], hot[0], preferred_element_type=f32), ALL_ROWS // 2)
    low0[...] = jnp.where((row & 1) == 1, pltpu.roll(both, 4, 0), both)

    for i in range(3):
        @pl.when(down)
        def _():
            top_copy(i).wait_recv()

    def main_block(b, _):
        at = pl.ds(pl.multiple_of(b * MAIN_BLOCK, MAIN_BLOCK), MAIN_BLOCK)
        upper = [held[c, :, at] for c in range(4)]
        lowest = [low0[:, at]]
        for i in range(3):
            level = top_recv[i, :, at].astype(f32)
            lowest.append(jnp.concatenate([level, level], axis=0))
        term = element_terms(upper, lowest, stretch[:, at], shear[:, at], thick[:, at], rate[:, at])
        abuf[:, at] = jnp.sum(fac[:, at] * term, axis=0, keepdims=True)
        bbuf[:, at] = jnp.sum(off[:, at] * term, axis=0, keepdims=True)
        return 0

    lax.fori_loop(0, corners.shape[1] // MAIN_BLOCK, main_block, 0)

    from_all(en_send, en_recv, en_s, en_r)
    for i in range(layers):
        for k in range(per):
            at = slice((i * per + k) * WIDE, (i * per + k + 1) * WIDE)
            abuf[:, at] = 0.25 * (abuf[:, at] * en_recv[i, k : k + 1, :] + bbuf[:, at])

    def scatter(c, count):
        def block(b, total):
            at = slice(b * SCATTER_BLOCK, (b + 1) * SCATTER_BLOCK)
            line = iota((2 * count, SCATTER_BLOCK), 0)
            high, low = split_bf16(abuf[:, at])
            value = jnp.where(line < count, high, low)
            place = jnp.where(line < count, line, line - count)
            spread = jnp.where(place == rows[c : c + 1, at], value, 0.0).astype(bf16)
            return total + lax.dot_general(hot[c, :, at], spread, (((1,), (1,)), ((), ())), preferred_element_type=f32)

        total = block(0, jnp.zeros((WIDE, 2 * count), f32)).T
        return total[0:count] + total[count : 2 * count]

    def ghost_sum(j):
        return remote(gh_send.at[j], gh_recv.at[3 - j], gh_s.at[j], gh_r.at[3 - j], g, p + OFFSETS[j])

    nodes = scatter(0, 24)
    for j in range(4):
        gh_send[j] = nodes[OWN_ROWS + j // 2 : OWN_ROWS + j // 2 + 1, (j % 2) * 128 : (j % 2 + 1) * 128]
    for j in range(4):
        @pl.when(valid[j])
        def _():
            ghost_sum(j).start()
    owned = nodes[0:OWN_ROWS]
    for c in range(1, 4):
        owned = owned + scatter(c, OWN_ROWS)
    owned = jnp.concatenate([owned[:, 0:128], owned[:, 128:256]], axis=0)

    for j in range(4):
        @pl.when(valid[j])
        def _():
            remote(gh_send.at[j], gh_recv.at[j], gh_s.at[j], gh_r.at[j], g, p + OFFSETS[j]).wait_recv()
    row64 = iota((64, 128), 0)
    added = None
    for d in range(4):
        ids = shared[d : d + 1, :]
        high, low = split_bf16(gh_recv[d])
        spread = jnp.where((row64 & 31) == (ids >> 7), jnp.where(row64 < 32, high, low), 0.0).astype(bf16)
        part = lax.dot_general(spread, one_hot(ids & 127, 128), (((1,), (1,)), ((), ())), preferred_element_type=f32)
        added = part if added is None else added + part
    owned = owned + (added[0:32] + added[32:64])

    core, chip, chips = lax.rem(g, 2), g // 2, layers // 2
    mate = g + 1 - 2 * core
    pair_send[0] = owned[0:16]
    pair_send[1] = owned[16:32]
    pair = remote(pair_send.at[1 - core], pair_recv, pair_s, pair_r, mate, p)
    pair.start()
    pair.wait_recv()
    all_recv[chip] = pair_send[core] + pair_recv[...]

    def over_chips(k):
        i = lax.rem(chip + k, chips)
        return remote(all_recv.at[chip], all_recv.at[chip], all_s.at[i], all_r.at[chip], 2 * i + core, p)

    def from_chip(k):
        i = lax.rem(chip + k, chips)
        return remote(all_recv.at[chip], all_recv.at[i], all_s.at[i], all_r.at[i], 2 * i + core, p)

    def start_chip(k, _):
        over_chips(far_first(k, chips)).start()
        return 0

    def wait_chip(k, _):
        from_chip(k).wait_recv()
        return 0

    lax.fori_loop(0, chips - 1, start_chip, 0)
    sent_all(sc_send, sc_recv, sc_s, sc_r)
    sent_all(en_send, en_recv, en_s, en_r)
    pair.wait_send()
    for j in range(4):
        @pl.when(valid[j])
        def _():
            ghost(j).wait_send()
            ghost_sum(j).wait_send()

        @pl.when(jnp.logical_and(valid[j], up))
        def _():
            low_ghost(j).wait_send()

    @pl.when(up)
    def _():
        low_copy.wait_send()
        for i in range(3):
            top_copy(i).wait_send()

    lax.fori_loop(1, chips, wait_chip, 0)
    total = all_recv[0]
    for i in range(1, chips):
        total = total + all_recv[i]
    done[core] = total
    last = remote(done.at[core], done.at[core], last_s, last_r, mate, p)
    last.start()
    remote(done.at[core], done.at[1 - core], last_s, last_r, mate, p).wait_recv()
    out[0:16] = done[0]
    out[16:32] = done[1]

    def sent_chip(k, _):
        over_chips(k).wait_send()
        return 0

    lax.fori_loop(1, chips, sent_chip, 0)
    last.wait_send()


def shards(layers, planes, *args):
    velocity, adjoint, corners, shared, stretch, shear_part, thickness, rate_factor, retention, weight = args
    per = OWN_ROWS // layers
    elems = corners.shape[1]
    f32, bf16 = jnp.float32, jnp.bfloat16
    vmem, dma = pltpu.VMEM, pltpu.SemaphoreType.DMA
    out = pl.pallas_call(
        functools.partial(kernel, layers, planes),
        out_shape=jax.ShapeDtypeStruct((32, 128), f32),
        in_specs=[pl.BlockSpec(memory_space=pltpu.HBM)] * 10,
        out_specs=pl.BlockSpec(memory_space=pltpu.VMEM),
        scratch_shapes=[vmem(a.shape, a.dtype) for a in args]
        + [
            vmem((OWN_ROWS * 32, WIDE), bf16), vmem((64, WIDE), bf16), vmem((80, WIDE), bf16),
            vmem((4, WIDE, elems), bf16), vmem((4, 32, elems), f32), vmem((4, elems), jnp.int32), vmem((8, elems), f32),
            vmem((3, 4, elems), bf16), vmem((3, 4, elems), bf16),
            vmem((64, WIDE), bf16), vmem((64, WIDE), bf16),
            vmem((4, 32, 128), bf16), vmem((4, 32, 128), bf16),
            vmem((4, 16, 128), bf16), vmem((4, 16, 128), bf16),
            vmem((8, elems), f32), vmem((8, elems), f32),
            vmem((layers, 2 * per, WIDE), f32), vmem((layers, 2 * per, WIDE), f32),
            vmem((layers, per, WIDE), f32), vmem((layers, per, WIDE), f32),
            vmem((1, elems), f32), vmem((1, elems), f32),
            vmem((4, 1, 128), f32), vmem((4, 1, 128), f32),
            vmem((2, 16, 128), f32), vmem((16, 128), f32), vmem((layers // 2, 16, 128), f32), vmem((2, 16, 128), f32),
            dma((10,)), dma, dma, dma((3,)), dma((3,)), dma((4,)), dma((4,)), dma((4,)), dma((4,)),
        ]
        + [dma((layers,)), dma((layers,)), dma((layers,)), dma((layers,)), dma((4,)), dma((4,)), dma, dma]
        + [dma((layers // 2,)), dma((layers // 2,)), dma, dma],
        compiler_params=pltpu.CompilerParams(collective_id=0, has_side_effects=True, vmem_limit_bytes=60 << 20),
        name="ice_gradient",
    )(*args)
    return out.reshape(4096)


def solution(mesh):
    return jax.shard_map(
        functools.partial(shards, mesh.shape["layer"], mesh.shape["plane"]),
        mesh=mesh,
        in_specs=(
            P(None, "layer", "plane"),
            P(None, "layer", "plane"),
            P(None, "plane"),
            P(None, "plane"),
            P(None, "plane"),
            P(None, "plane"),
            P("layer", "plane"),
            P("layer", "plane"),
            P("layer", "plane"),
            P("layer", "plane"),
        ),
        out_specs=P("plane"),
        check_vma=False,
    )
```

```python
import functools
import math

import jax
import jax.numpy as jnp
from jax import lax
from jax.experimental import pallas as pl
from jax.experimental.pallas import tpu as pltpu
from jax.sharding import PartitionSpec as P

OFFSETS = (-2, -1, 1, 2)
STRAIN_EPS = 0.01
GAUSS = 1.0 / math.sqrt(3.0)
MESH = pl.DeviceIdType.MESH
WIDE = 256
HALF = 2048
OWN_ROWS = 16
ALL_ROWS = 18
MAIN_BLOCK = 512
SCATTER_BLOCK = 4096


def far_first(k, count):
    return count // 2 + (k + 1) // 2 * (2 * lax.rem(k, 2) - 1)


def iota(shape, axis):
    return lax.broadcasted_iota(jnp.int32, shape, axis)


def one_hot(low, width):
    return (iota((width, low.shape[1]), 0) == low).astype(jnp.float32).astype(jnp.bfloat16)


def place_of(ids):
    owned = ids < 2 * HALF
    row = jnp.where(owned, (ids >> 7) & 15, ids >> 8)
    spot = jnp.where(owned, (ids & 127) | ((ids >> 4) & 128), ids & 255)
    return row, spot


def owned_row(ref, lead, i):
    return jnp.concatenate([ref[lead, :, i * 128 : (i + 1) * 128], ref[lead, :, HALF + i * 128 : HALF + (i + 1) * 128]], axis=1)


def pick(row, size, table, count):
    out = table[0:size]
    for i in range(1, count):
        out = jnp.where(row == i, table[i * size : (i + 1) * size], out)
    return out


def corner_modes(v):
    p, q, r, s = v[1] - v[0], v[2] - v[3], v[0] + v[1], v[2] + v[3]
    return r + s, p + q, s - r, q - p


def element_terms(upper, lowest, stretch, shear, thick, rate):
    n = thick.shape[1]
    last = iota((8, n), 0) == 7
    top, end = corner_modes(upper), corner_modes(lowest)
    derived = []
    for comp in range(4):
        half, diff = [], []
        for m in range(4):
            t = top[m][comp * 8 : (comp + 1) * 8]
            b = jnp.where(last, pltpu.roll(end[m], 7 - comp, 0), pltpu.roll(t, 7, 0))
            d = t - b
            diff.append(d)
            if m:
                mean = t + b
                gd = GAUSS * d
                half.append((mean - gd, mean + gd))
        mx, my, mxy = half
        xi, eta = [], []
        for z in range(2):
            t = GAUSS * mxy[z]
            xi.append((mx[z] - t, mx[z] + t))
            eta.append((my[z] - t, my[z] + t))
        d0, dx, dy, dxy = diff
        gx, gy, gxy = GAUSS * dx, GAUSS * dy, (GAUSS * GAUSS) * dxy
        a0, a1, b0, b1 = d0 - gx, d0 + gx, gy - gxy, gy + gxy
        derived.append((xi, eta, ((a0 - b0, a0 + b0), (a1 - b1, a1 + b1))))
    s0, s1 = 0.125 * stretch[0:1], 0.125 * stretch[1:2]
    h0, h1 = 0.125 * shear[0:1], 0.125 * shear[1:2]
    inv = 0.125 / thick

    def strains(first, second):
        axi, aeta, az = derived[first]
        bxi, beta, bz = derived[second]
        two = range(2)
        return (
            [[s0 * axi[z][e] for e in two] for z in two],
            [[h0 * aeta[z][x] for x in two] for z in two],
            [[h1 * bxi[z][e] for e in two] for z in two],
            [[s1 * beta[z][x] for x in two] for z in two],
            [[h1 * axi[z][e] + s0 * bxi[z][e] for e in two] for z in two],
            [[s1 * aeta[z][x] + h0 * beta[z][x] for x in two] for z in two],
            [[inv * az[x][e] for e in two] for x in two],
            [[inv * bz[x][e] for e in two] for x in two],
        )

    f, g = strains(0, 1), strains(2, 3)
    total = None
    for x in range(2):
        for e in range(2):
            fxz, fyz, gxz, gyz = f[6][x][e], f[7][x][e], g[6][x][e], g[7][x][e]
            own_z = fxz * fxz + fyz * fyz + STRAIN_EPS
            cross_z = fxz * gxz + fyz * gyz
            for z in range(2):
                fxx, fyy = f[0][z][e] + f[1][z][x], f[2][z][e] + f[3][z][x]
                fxy = 0.5 * (f[4][z][e] + f[5][z][x])
                gxx, gyy = g[0][z][e] + g[1][z][x], g[2][z][e] + g[3][z][x]
                gxy = 0.5 * (g[4][z][e] + g[5][z][x])
                a, b = fxx + 0.5 * fyy, fyy + 0.5 * fxx
                effective = fxx * a + fyy * b + fxy * fxy + own_z
                cross = gxx * a + gyy * b + fxy * gxy + cross_z
                term = jnp.exp2((-1.0 / 3.0) * jnp.log2(effective)) * cross
                total = term if total is None else total + term
    det = stretch[0:1] * stretch[1:2] - shear[0:1] * shear[1:2]
    return (rate * thick) * (total / det)


def recurrence(keep, wei):
    sub = iota(keep.shape, 0)
    factor, offset = keep, (1.0 - keep) * wei
    for d in (1, 2, 4):
        before_f = jnp.where(sub >= d, pltpu.roll(factor, d, 0), 1.0)
        before_o = jnp.where(sub >= d, pltpu.roll(offset, d, 0), 0.0)
        offset = factor * before_o + offset
        factor = factor * before_f
    return factor, offset


def split_bf16(x):
    high = x.astype(jnp.bfloat16).astype(jnp.float32)
    return high, x - high


def kernel(
    layers,
    planes,
    vel_hbm, adj_hbm, cor_hbm, sha_hbm, str_hbm, she_hbm, thi_hbm, rat_hbm, ret_hbm, wei_hbm,
    out,
    vel, adj, corners, shared, stretch, shear, thick, rate, ret, wei,
    table, late, late8, hot, held, rows, low0, top_send, top_recv, low_send, low_own, gsend, grecv, lsend, lrecv,
    fac, off, sc_send, sc_recv, en_send, en_recv,
    abuf, bbuf,
    gh_send, gh_recv, pair_send, pair_recv, all_recv, done,
    in_sem, low_s, low_r, top_s, top_r, g_s, g_r, l_s, l_r, sc_s, sc_r, en_s, en_r, gh_s, gh_r, pair_s, pair_r, all_s, all_r, last_s, last_r,
):
    g, p = lax.axis_index("layer"), lax.axis_index("plane")
    per = OWN_ROWS // layers
    f32, bf16 = jnp.float32, jnp.bfloat16

    hbm = (vel_hbm, adj_hbm, sha_hbm, ret_hbm, wei_hbm, cor_hbm, str_hbm, she_hbm, thi_hbm, rat_hbm)
    own = (vel, adj, shared, ret, wei, corners, stretch, shear, thick, rate)
    loads = [pltpu.make_async_copy(a, b, in_sem.at[i]) for i, (a, b) in enumerate(zip(hbm, own))]
    for load in loads:
        load.start()

    valid = [jnp.logical_and(p + o >= 0, p + o < planes) for o in OFFSETS]
    up, down = g > 0, g < layers - 1

    for d in range(4):
        @pl.when(jnp.logical_not(valid[d]))
        def _():
            grecv[d] = jnp.zeros(grecv.shape[1:], bf16)
            lrecv[d] = jnp.zeros(lrecv.shape[1:], bf16)
            gh_recv[0, d] = jnp.zeros(gh_recv.shape[2:], f32)
            gh_recv[1, d] = jnp.zeros(gh_recv.shape[2:], f32)

    @pl.when(jnp.logical_not(down))
    def _():
        low_own[...] = jnp.zeros(low_own.shape, bf16)
        lrecv[...] = jnp.zeros(lrecv.shape, bf16)
        top_recv[...] = jnp.zeros(top_recv.shape, bf16)

    barrier = pltpu.get_barrier_semaphore()

    def greet(layer, plane):
        pl.semaphore_signal(barrier, inc=1, device_id=(layer, plane), device_id_type=MESH)

    def greet_layer(r, _):
        greet(lax.rem(g + r, layers), p)
        return 0

    lax.fori_loop(1, layers, greet_layer, 0)
    expected = layers - 1
    for d, o in enumerate(OFFSETS):
        @pl.when(valid[d])
        def _():
            greet(g, p + o)

        @pl.when(jnp.logical_and(valid[d], up))
        def _():
            greet(g - 1, p + o)

        @pl.when(jnp.logical_and(valid[d], down))
        def _():
            greet(g + 1, p + o)

        expected = expected + valid[d].astype(jnp.int32) * (1 + up.astype(jnp.int32) + down.astype(jnp.int32))

    loads[0].wait()
    loads[1].wait()
    for i in range(OWN_ROWS):
        table[i * 32 : (i + 1) * 32] = jnp.concatenate([owned_row(f, k, i) for f in (vel, adj) for k in range(2)], axis=0)
    row8 = iota((8, WIDE), 0)
    pieces = []
    for i in range(0, OWN_ROWS, 2):
        piece = jnp.zeros((8, WIDE), f32)
        for half in range(2):
            for comp in range(4):
                level = owned_row((vel, adj)[comp // 2], comp % 2, i + half).astype(f32)
                piece = jnp.where(row8 == half * 4 + comp, level[0:1], piece)
        pieces.append(piece)
    low_send[...] = jnp.concatenate(pieces, axis=0).astype(bf16)
    loads[2].wait()
    row16 = iota((16, 128), 0)
    for j in range(4):
        ids = shared[j : j + 1, :]
        row, spot = place_of(ids)
        sent = jnp.dot(table[...], one_hot(spot, WIDE), preferred_element_type=f32)
        sent = pick(row, 32, sent, OWN_ROWS)
        gsend[j] = sent.astype(bf16)
        tops = jnp.zeros((16, 128), f32)
        for comp in range(4):
            tops = jnp.where(row16 == comp, sent[comp * 8 : comp * 8 + 1], tops)
        lsend[j] = tops.astype(bf16)
    loads[3].wait()
    loads[4].wait()
    for i in range(8):
        at = slice(i * 512, (i + 1) * 512)
        factor, offset = recurrence(ret[:, at], wei[:, at])
        fac[:, at] = factor
        off[:, at] = offset
    for i in range(layers):
        for k in range(per):
            at = slice((i * per + k) * WIDE, (i * per + k + 1) * WIDE)
            sc_send[i, k : k + 1, :] = fac[7:8, at]
            sc_send[i, per + k : per + k + 1, :] = off[7:8, at]

    pl.semaphore_wait(barrier, expected)

    def remote(src, dst, s, r, layer, plane):
        return pltpu.make_async_remote_copy(
            src_ref=src, dst_ref=dst, send_sem=s, recv_sem=r, device_id=(layer, plane), device_id_type=MESH
        )

    def to_all(send, recv, s, r):
        def copy(i):
            return remote(send.at[i], recv.at[g], s.at[i], r.at[g], i, p)

        def start(k, _):
            copy(lax.rem(g + far_first(k, layers), layers)).start()
            return 0

        lax.fori_loop(0, layers - 1, start, 0)

    def from_all(send, recv, s, r):
        def wait(k, _):
            i = lax.rem(g + k, layers)
            remote(send.at[i], recv.at[i], s.at[i], r.at[i], i, p).wait_recv()
            return 0

        lax.fori_loop(1, layers, wait, 0)

    def sent_all(send, recv, s, r):
        def wait(k, _):
            i = lax.rem(g + k, layers)
            remote(send.at[i], recv.at[i], s.at[i], r.at[i], i, p).wait_send()
            return 0

        lax.fori_loop(1, layers, wait, 0)

    def ghost(j):
        return remote(gsend.at[j], grecv.at[3 - j], g_s.at[j], g_r.at[3 - j], g, p + OFFSETS[j])

    def low_ghost(j):
        return remote(lsend.at[j], lrecv.at[3 - j], l_s.at[j], l_r.at[3 - j], g - 1, p + OFFSETS[j])

    low_copy = remote(low_send, low_own, low_s, low_r, g - 1, p)

    to_all(sc_send, sc_recv, sc_s, sc_r)

    for j in range(4):
        @pl.when(valid[j])
        def _():
            ghost(j).start()

        @pl.when(jnp.logical_and(valid[j], up))
        def _():
            low_ghost(j).start()

    @pl.when(up)
    def _():
        low_copy.start()

    def top_copy(i):
        return remote(top_send.at[i], top_recv.at[i], top_s.at[i], top_r.at[i], g - 1, p)

    def enter():
        sc_recv[g] = sc_send[g]
        from_all(sc_send, sc_recv, sc_s, sc_r)
        running = jnp.zeros((per, WIDE), f32)
        for i in range(layers):
            en_send[i] = running
            running = sc_recv[i, 0:per, :] * running + sc_recv[i, per : 2 * per, :]
        to_all(en_send, en_recv, en_s, en_r)
        en_recv[g] = en_send[g]

    def gather(b, _):
        @pl.when(b == 3)
        def _():
            enter()

        c = lax.rem(b + 1, 4)
        row, spot = place_of(corners[pl.ds(c, 1), :])
        spot = one_hot(spot, WIDE)
        rows[pl.ds(c, 1), :] = row
        hot[c] = spot
        found = pick(row, 32, jnp.dot(table[...], spot, preferred_element_type=f32), OWN_ROWS)
        held[c] = found

        @pl.when(jnp.logical_and(b < 3, up))
        def _():
            top_send[b] = jnp.concatenate([found[8 * k : 8 * k + 1] for k in range(4)], axis=0).astype(bf16)
            top_copy(b).start()

        return 0

    loads[5].wait()
    lax.fori_loop(0, 4, gather, 0)

    for load in loads[6:]:
        load.wait()

    for j in range(4):
        @pl.when(valid[j])
        def _():
            remote(gsend.at[j], grecv.at[j], g_s.at[j], g_r.at[j], g, p + OFFSETS[j]).wait_recv()

        @pl.when(jnp.logical_and(valid[j], down))
        def _():
            remote(lsend.at[j], lrecv.at[j], l_s.at[j], l_r.at[j], g, p + OFFSETS[j]).wait_recv()

    @pl.when(down)
    def _():
        low_copy.wait_recv()

    for i in range(2):
        late[i * 32 : (i + 1) * 32] = jnp.concatenate([grecv[2 * i], grecv[2 * i + 1]], axis=1)
    late8[0:64] = low_own[...]
    first = jnp.concatenate([lrecv[0], lrecv[1]], axis=1).astype(f32)[0:8]
    second = jnp.concatenate([lrecv[2], lrecv[3]], axis=1).astype(f32)[0:8]
    ghosts8 = first + pltpu.roll(second, 4, 0)
    late8[64:80] = jnp.concatenate([ghosts8, jnp.zeros((8, WIDE), f32)], axis=0).astype(bf16)

    row = rows[0:1, :]
    found = jnp.dot(late[...], hot[0], preferred_element_type=f32)
    held[0] = jnp.where(row == 17, found[32:64], jnp.where(row == 16, found[0:32], held[0]))
    both = pick(row >> 1, 8, jnp.dot(late8[...], hot[0], preferred_element_type=f32), ALL_ROWS // 2)
    low0[...] = jnp.where((row & 1) == 1, pltpu.roll(both, 4, 0), both)

    for i in range(3):
        @pl.when(down)
        def _():
            top_copy(i).wait_recv()

    def main_block(b, _):
        at = pl.ds(pl.multiple_of(b * MAIN_BLOCK, MAIN_BLOCK), MAIN_BLOCK)
        upper = [held[c, :, at] for c in range(4)]
        lowest = [low0[:, at]]
        for i in range(3):
            level = top_recv[i, :, at].astype(f32)
            lowest.append(jnp.concatenate([level, level], axis=0))
        term = element_terms(upper, lowest, stretch[:, at], shear[:, at], thick[:, at], rate[:, at])
        abuf[:, at] = jnp.sum(fac[:, at] * term, axis=0, keepdims=True)
        bbuf[:, at] = jnp.sum(off[:, at] * term, axis=0, keepdims=True)
        return 0

    lax.fori_loop(0, corners.shape[1] // MAIN_BLOCK, main_block, 0)

    from_all(en_send, en_recv, en_s, en_r)
    for i in range(layers):
        for k in range(per):
            at = slice((i * per + k) * WIDE, (i * per + k + 1) * WIDE)
            abuf[:, at] = 0.25 * (abuf[:, at] * en_recv[i, k : k + 1, :] + bbuf[:, at])

    def scatter(c, count):
        def block(b, total):
            at = slice(b * SCATTER_BLOCK, (b + 1) * SCATTER_BLOCK)
            line = iota((2 * count, SCATTER_BLOCK), 0)
            high, low = split_bf16(abuf[:, at])
            value = jnp.where(line < count, high, low)
            place = jnp.where(line < count, line, line - count)
            spread = jnp.where(place == rows[c : c + 1, at], value, 0.0).astype(bf16)
            return total + lax.dot_general(hot[c, :, at], spread, (((1,), (1,)), ((), ())), preferred_element_type=f32)

        total = block(0, jnp.zeros((WIDE, 2 * count), f32)).T
        return total[0:count] + total[count : 2 * count]

    core, chip, chips = lax.rem(g, 2), g // 2, layers // 2
    mate = g + 1 - 2 * core

    def ghost_sum(j, other):
        to = mate if other else g
        return remote(gh_send.at[j], gh_recv.at[core, 3 - j], gh_s.at[other, j], gh_r.at[core, 3 - j], to, p + OFFSETS[j])

    def ghost_from(j, k):
        return remote(gh_send.at[j], gh_recv.at[k, j], gh_s.at[0, j], gh_r.at[k, j], g, p + OFFSETS[j])

    nodes = scatter(0, 24)
    for j in range(4):
        gh_send[j] = nodes[OWN_ROWS + j // 2 : OWN_ROWS + j // 2 + 1, (j % 2) * 128 : (j % 2 + 1) * 128]
    for j in range(4):
        @pl.when(valid[j])
        def _():
            ghost_sum(j, 0).start()
            ghost_sum(j, 1).start()
    owned = nodes[0:OWN_ROWS]
    for c in range(1, 4):
        owned = owned + scatter(c, OWN_ROWS)
    owned = jnp.concatenate([owned[:, 0:128], owned[:, 128:256]], axis=0)

    pair_send[0] = owned[0:16]
    pair_send[1] = owned[16:32]
    pair = remote(pair_send.at[1 - core], pair_recv, pair_s, pair_r, mate, p)
    pair.start()

    line32 = iota((32, 512), 0)
    ids = jnp.concatenate([shared[d : d + 1, :] for d in range(4)], axis=1)
    hots = one_hot(ids & 127, 128)
    spots = (line32 & 15) + 16 * core == (ids >> 7)
    pair.wait_recv()
    for j in range(4):
        @pl.when(valid[j])
        def _():
            ghost_from(j, 0).wait_recv()
            ghost_from(j, 1).wait_recv()

    high, low = split_bf16(jnp.concatenate([gh_recv[0, d] + gh_recv[1, d] for d in range(4)], axis=1))
    spread = jnp.where(spots, jnp.where(line32 < 16, high, low), 0.0).astype(bf16)
    added = lax.dot_general(spread, hots, (((1,), (1,)), ((), ())), preferred_element_type=f32)
    all_recv[chip] = (pair_send[core] + pair_recv[...]) + (added[0:16] + added[16:32])

    def over_chips(k):
        i = lax.rem(chip + k, chips)
        return remote(all_recv.at[chip], all_recv.at[chip], all_s.at[i], all_r.at[chip], 2 * i + core, p)

    def from_chip(k):
        i = lax.rem(chip + k, chips)
        return remote(all_recv.at[chip], all_recv.at[i], all_s.at[i], all_r.at[i], 2 * i + core, p)

    def start_chip(k, _):
        over_chips(far_first(k, chips)).start()
        return 0

    def wait_chip(k, _):
        from_chip(k).wait_recv()
        return 0

    lax.fori_loop(0, chips - 1, start_chip, 0)
    sent_all(sc_send, sc_recv, sc_s, sc_r)
    sent_all(en_send, en_recv, en_s, en_r)
    pair.wait_send()
    for j in range(4):
        @pl.when(valid[j])
        def _():
            ghost(j).wait_send()
            ghost_sum(j, 0).wait_send()
            ghost_sum(j, 1).wait_send()

        @pl.when(jnp.logical_and(valid[j], up))
        def _():
            low_ghost(j).wait_send()

    @pl.when(up)
    def _():
        low_copy.wait_send()
        for i in range(3):
            top_copy(i).wait_send()

    lax.fori_loop(1, chips, wait_chip, 0)
    total = all_recv[0]
    for i in range(1, chips):
        total = total + all_recv[i]
    done[core] = total
    last = remote(done.at[core], done.at[core], last_s, last_r, mate, p)
    last.start()
    remote(done.at[core], done.at[1 - core], last_s, last_r, mate, p).wait_recv()
    out[0:16] = done[0]
    out[16:32] = done[1]

    def sent_chip(k, _):
        over_chips(k).wait_send()
        return 0

    lax.fori_loop(1, chips, sent_chip, 0)
    last.wait_send()


def shards(layers, planes, *args):
    velocity, adjoint, corners, shared, stretch, shear_part, thickness, rate_factor, retention, weight = args
    per = OWN_ROWS // layers
    elems = corners.shape[1]
    f32, bf16 = jnp.float32, jnp.bfloat16
    vmem, dma = pltpu.VMEM, pltpu.SemaphoreType.DMA
    out = pl.pallas_call(
        functools.partial(kernel, layers, planes),
        out_shape=jax.ShapeDtypeStruct((32, 128), f32),
        in_specs=[pl.BlockSpec(memory_space=pltpu.HBM)] * 10,
        out_specs=pl.BlockSpec(memory_space=pltpu.VMEM),
        scratch_shapes=[vmem(a.shape, a.dtype) for a in args]
        + [
            vmem((OWN_ROWS * 32, WIDE), bf16), vmem((64, WIDE), bf16), vmem((80, WIDE), bf16),
            vmem((4, WIDE, elems), bf16), vmem((4, 32, elems), f32), vmem((4, elems), jnp.int32), vmem((8, elems), f32),
            vmem((3, 4, elems), bf16), vmem((3, 4, elems), bf16),
            vmem((64, WIDE), bf16), vmem((64, WIDE), bf16),
            vmem((4, 32, 128), bf16), vmem((4, 32, 128), bf16),
            vmem((4, 16, 128), bf16), vmem((4, 16, 128), bf16),
            vmem((8, elems), f32), vmem((8, elems), f32),
            vmem((layers, 2 * per, WIDE), f32), vmem((layers, 2 * per, WIDE), f32),
            vmem((layers, per, WIDE), f32), vmem((layers, per, WIDE), f32),
            vmem((1, elems), f32), vmem((1, elems), f32),
            vmem((4, 1, 128), f32), vmem((2, 4, 1, 128), f32),
            vmem((2, 16, 128), f32), vmem((16, 128), f32), vmem((layers // 2, 16, 128), f32), vmem((2, 16, 128), f32),
            dma((10,)), dma, dma, dma((3,)), dma((3,)), dma((4,)), dma((4,)), dma((4,)), dma((4,)),
        ]
        + [dma((layers,)), dma((layers,)), dma((layers,)), dma((layers,)), dma((2, 4)), dma((2, 4)), dma, dma]
        + [dma((layers // 2,)), dma((layers // 2,)), dma, dma],
        compiler_params=pltpu.CompilerParams(collective_id=0, has_side_effects=True, vmem_limit_bytes=60 << 20),
        name="ice_gradient",
    )(*args)
    return out.reshape(4096)


def solution(mesh):
    return jax.shard_map(
        functools.partial(shards, mesh.shape["layer"], mesh.shape["plane"]),
        mesh=mesh,
        in_specs=(
            P(None, "layer", "plane"),
            P(None, "layer", "plane"),
            P(None, "plane"),
            P(None, "plane"),
            P(None, "plane"),
            P(None, "plane"),
            P("layer", "plane"),
            P("layer", "plane"),
            P("layer", "plane"),
            P("layer", "plane"),
        ),
        out_specs=P("plane"),
        check_vma=False,
    )
```

```python
import functools
import math

import jax
import jax.numpy as jnp
from jax import lax
from jax.experimental import pallas as pl
from jax.experimental.pallas import tpu as pltpu
from jax.sharding import PartitionSpec as P

OFFSETS = (-2, -1, 1, 2)
STRAIN_EPS = 0.01
GAUSS = 1.0 / math.sqrt(3.0)
MESH = pl.DeviceIdType.MESH
WIDE = 256
HALF = 2048
OWN_ROWS = 16
ALL_ROWS = 18
MAIN_BLOCK = 512
SCATTER_BLOCK = 4096


def far_first(k, count):
    return count // 2 + (k + 1) // 2 * (2 * lax.rem(k, 2) - 1)


def iota(shape, axis):
    return lax.broadcasted_iota(jnp.int32, shape, axis)


def one_hot(low, width):
    return (iota((width, low.shape[1]), 0) == low).astype(jnp.float32).astype(jnp.bfloat16)


def place_of(ids):
    owned = ids < 2 * HALF
    row = jnp.where(owned, (ids >> 7) & 15, ids >> 8)
    spot = jnp.where(owned, (ids & 127) | ((ids >> 4) & 128), ids & 255)
    return row, spot


def owned_row(ref, lead, i):
    return jnp.concatenate([ref[lead, :, i * 128 : (i + 1) * 128], ref[lead, :, HALF + i * 128 : HALF + (i + 1) * 128]], axis=1)


def pick(row, size, table, count):
    out = table[0:size]
    for i in range(1, count):
        out = jnp.where(row == i, table[i * size : (i + 1) * size], out)
    return out


def corner_modes(v):
    p, q, r, s = v[1] - v[0], v[2] - v[3], v[0] + v[1], v[2] + v[3]
    return r + s, p + q, s - r, q - p


def element_terms(upper, lowest, stretch, shear, thick, rate):
    n = thick.shape[1]
    last = iota((8, n), 0) == 7
    top, end = corner_modes(upper), corner_modes(lowest)
    derived = []
    for comp in range(4):
        half, diff = [], []
        for m in range(4):
            t = top[m][comp * 8 : (comp + 1) * 8]
            b = jnp.where(last, pltpu.roll(end[m], 7 - comp, 0), pltpu.roll(t, 7, 0))
            d = t - b
            diff.append(d)
            if m:
                mean = t + b
                gd = GAUSS * d
                half.append((mean - gd, mean + gd))
        mx, my, mxy = half
        xi, eta = [], []
        for z in range(2):
            t = GAUSS * mxy[z]
            xi.append((mx[z] - t, mx[z] + t))
            eta.append((my[z] - t, my[z] + t))
        d0, dx, dy, dxy = diff
        gx, gy, gxy = GAUSS * dx, GAUSS * dy, (GAUSS * GAUSS) * dxy
        a0, a1, b0, b1 = d0 - gx, d0 + gx, gy - gxy, gy + gxy
        derived.append((xi, eta, ((a0 - b0, a0 + b0), (a1 - b1, a1 + b1))))
    s0, s1 = 0.125 * stretch[0:1], 0.125 * stretch[1:2]
    h0, h1 = 0.125 * shear[0:1], 0.125 * shear[1:2]
    inv = 0.125 / thick

    def strains(first, second):
        axi, aeta, az = derived[first]
        bxi, beta, bz = derived[second]
        two = range(2)
        return (
            [[s0 * axi[z][e] for e in two] for z in two],
            [[h0 * aeta[z][x] for x in two] for z in two],
            [[h1 * bxi[z][e] for e in two] for z in two],
            [[s1 * beta[z][x] for x in two] for z in two],
            [[h1 * axi[z][e] + s0 * bxi[z][e] for e in two] for z in two],
            [[s1 * aeta[z][x] + h0 * beta[z][x] for x in two] for z in two],
            [[inv * az[x][e] for e in two] for x in two],
            [[inv * bz[x][e] for e in two] for x in two],
        )

    f, g = strains(0, 1), strains(2, 3)
    total = None
    for x in range(2):
        for e in range(2):
            fxz, fyz, gxz, gyz = f[6][x][e], f[7][x][e], g[6][x][e], g[7][x][e]
            own_z = fxz * fxz + fyz * fyz + STRAIN_EPS
            cross_z = fxz * gxz + fyz * gyz
            for z in range(2):
                fxx, fyy = f[0][z][e] + f[1][z][x], f[2][z][e] + f[3][z][x]
                fxy = 0.5 * (f[4][z][e] + f[5][z][x])
                gxx, gyy = g[0][z][e] + g[1][z][x], g[2][z][e] + g[3][z][x]
                gxy = 0.5 * (g[4][z][e] + g[5][z][x])
                a, b = fxx + 0.5 * fyy, fyy + 0.5 * fxx
                effective = fxx * a + fyy * b + fxy * fxy + own_z
                cross = gxx * a + gyy * b + fxy * gxy + cross_z
                term = jnp.exp2((-1.0 / 3.0) * jnp.log2(effective)) * cross
                total = term if total is None else total + term
    det = stretch[0:1] * stretch[1:2] - shear[0:1] * shear[1:2]
    return (rate * thick) * (total / det)


def recurrence(keep, wei):
    sub = iota(keep.shape, 0)
    factor, offset = keep, (1.0 - keep) * wei
    for d in (1, 2, 4):
        before_f = jnp.where(sub >= d, pltpu.roll(factor, d, 0), 1.0)
        before_o = jnp.where(sub >= d, pltpu.roll(offset, d, 0), 0.0)
        offset = factor * before_o + offset
        factor = factor * before_f
    return factor, offset


def split_bf16(x):
    high = x.astype(jnp.bfloat16).astype(jnp.float32)
    return high, x - high


def kernel(
    layers,
    planes,
    vel_hbm, adj_hbm, cor_hbm, sha_hbm, str_hbm, she_hbm, thi_hbm, rat_hbm, ret_hbm, wei_hbm,
    out,
    vel, adj, corners, shared, stretch, shear, thick, rate, ret, wei,
    table, late, late8, hot, held, rows, low0, top_send, top_recv, low_send, low_own, gsend, grecv, lsend, lrecv,
    fac, off, sc_send, sc_recv, en_send, en_recv,
    abuf, bbuf,
    gh_send, gh_recv, pair_send, pair_recv, all_recv, done,
    in_sem, low_s, low_r, top_s, top_r, g_s, g_r, l_s, l_r, sc_s, sc_r, en_s, en_r, gh_s, gh_r, pair_s, pair_r, all_s, all_r, last_s, last_r,
):
    g, p = lax.axis_index("layer"), lax.axis_index("plane")
    per = OWN_ROWS // layers
    f32, bf16 = jnp.float32, jnp.bfloat16

    hbm = (vel_hbm, adj_hbm, sha_hbm, ret_hbm, wei_hbm, cor_hbm, str_hbm, she_hbm, thi_hbm, rat_hbm)
    own = (vel, adj, shared, ret, wei, corners, stretch, shear, thick, rate)
    loads = [pltpu.make_async_copy(a, b, in_sem.at[i]) for i, (a, b) in enumerate(zip(hbm, own))]
    for load in loads:
        load.start()

    valid = [jnp.logical_and(p + o >= 0, p + o < planes) for o in OFFSETS]
    up, down = g > 0, g < layers - 1

    for d in range(4):
        @pl.when(jnp.logical_not(valid[d]))
        def _():
            grecv[d] = jnp.zeros(grecv.shape[1:], bf16)
            lrecv[d] = jnp.zeros(lrecv.shape[1:], bf16)
            gh_recv[0, d] = jnp.zeros(gh_recv.shape[2:], f32)
            gh_recv[1, d] = jnp.zeros(gh_recv.shape[2:], f32)

    @pl.when(jnp.logical_not(down))
    def _():
        low_own[...] = jnp.zeros(low_own.shape, bf16)
        lrecv[...] = jnp.zeros(lrecv.shape, bf16)
        top_recv[...] = jnp.zeros(top_recv.shape, bf16)

    barrier = pltpu.get_barrier_semaphore()

    def greet(layer, plane):
        pl.semaphore_signal(barrier, inc=1, device_id=(layer, plane), device_id_type=MESH)

    def greet_layer(r, _):
        greet(lax.rem(g + r, layers), p)
        return 0

    lax.fori_loop(1, layers, greet_layer, 0)
    expected = layers - 1
    for d, o in enumerate(OFFSETS):
        @pl.when(valid[d])
        def _():
            greet(g, p + o)

        @pl.when(jnp.logical_and(valid[d], up))
        def _():
            greet(g - 1, p + o)

        @pl.when(jnp.logical_and(valid[d], down))
        def _():
            greet(g + 1, p + o)

        expected = expected + valid[d].astype(jnp.int32) * (1 + up.astype(jnp.int32) + down.astype(jnp.int32))

    loads[0].wait()
    loads[1].wait()
    for i in range(OWN_ROWS):
        table[i * 32 : (i + 1) * 32] = jnp.concatenate([owned_row(f, k, i) for f in (vel, adj) for k in range(2)], axis=0)
    row8 = iota((8, WIDE), 0)
    pieces = []
    for i in range(0, OWN_ROWS, 2):
        piece = jnp.zeros((8, WIDE), f32)
        for half in range(2):
            for comp in range(4):
                level = owned_row((vel, adj)[comp // 2], comp % 2, i + half).astype(f32)
                piece = jnp.where(row8 == half * 4 + comp, level[0:1], piece)
        pieces.append(piece)
    low_send[...] = jnp.concatenate(pieces, axis=0).astype(bf16)
    loads[2].wait()
    row16 = iota((16, 128), 0)
    for j in range(4):
        ids = shared[j : j + 1, :]
        row, spot = place_of(ids)
        sent = jnp.dot(table[...], one_hot(spot, WIDE), preferred_element_type=f32)
        sent = pick(row, 32, sent, OWN_ROWS)
        gsend[j] = sent.astype(bf16)
        tops = jnp.zeros((16, 128), f32)
        for comp in range(4):
            tops = jnp.where(row16 == comp, sent[comp * 8 : comp * 8 + 1], tops)
        lsend[j] = tops.astype(bf16)
    loads[3].wait()
    loads[4].wait()
    for i in range(8):
        at = slice(i * 512, (i + 1) * 512)
        factor, offset = recurrence(ret[:, at], wei[:, at])
        fac[:, at] = factor
        off[:, at] = offset
    for i in range(layers):
        for k in range(per):
            at = slice((i * per + k) * WIDE, (i * per + k + 1) * WIDE)
            sc_send[i, k : k + 1, :] = fac[7:8, at]
            sc_send[i, per + k : per + k + 1, :] = off[7:8, at]

    pl.semaphore_wait(barrier, expected)

    def remote(src, dst, s, r, layer, plane):
        return pltpu.make_async_remote_copy(
            src_ref=src, dst_ref=dst, send_sem=s, recv_sem=r, device_id=(layer, plane), device_id_type=MESH
        )

    def to_all(send, recv, s, r):
        def copy(i):
            return remote(send.at[i], recv.at[g], s.at[i], r.at[g], i, p)

        def start(k, _):
            copy(lax.rem(g + far_first(k, layers), layers)).start()
            return 0

        lax.fori_loop(0, layers - 1, start, 0)

    def from_all(send, recv, s, r):
        def wait(k, _):
            i = lax.rem(g + k, layers)
            remote(send.at[i], recv.at[i], s.at[i], r.at[i], i, p).wait_recv()
            return 0

        lax.fori_loop(1, layers, wait, 0)

    def sent_all(send, recv, s, r):
        def wait(k, _):
            i = lax.rem(g + k, layers)
            remote(send.at[i], recv.at[i], s.at[i], r.at[i], i, p).wait_send()
            return 0

        lax.fori_loop(1, layers, wait, 0)

    def ghost(j):
        return remote(gsend.at[j], grecv.at[3 - j], g_s.at[j], g_r.at[3 - j], g, p + OFFSETS[j])

    def low_ghost(j):
        return remote(lsend.at[j], lrecv.at[3 - j], l_s.at[j], l_r.at[3 - j], g - 1, p + OFFSETS[j])

    low_copy = remote(low_send, low_own, low_s, low_r, g - 1, p)

    to_all(sc_send, sc_recv, sc_s, sc_r)

    for j in range(4):
        @pl.when(valid[j])
        def _():
            ghost(j).start()

        @pl.when(jnp.logical_and(valid[j], up))
        def _():
            low_ghost(j).start()

    @pl.when(up)
    def _():
        low_copy.start()

    def top_copy(i):
        return remote(top_send.at[i], top_recv.at[i], top_s.at[i], top_r.at[i], g - 1, p)

    def enter():
        sc_recv[g] = sc_send[g]
        from_all(sc_send, sc_recv, sc_s, sc_r)
        running = jnp.zeros((per, WIDE), f32)
        for i in range(layers):
            en_send[i] = running
            running = sc_recv[i, 0:per, :] * running + sc_recv[i, per : 2 * per, :]
        to_all(en_send, en_recv, en_s, en_r)
        en_recv[g] = en_send[g]

    def gather(b, _):
        @pl.when(b == 3)
        def _():
            enter()

        c = lax.rem(b + 1, 4)
        row, spot = place_of(corners[pl.ds(c, 1), :])
        spot = one_hot(spot, WIDE)
        rows[pl.ds(c, 1), :] = row
        hot[c] = spot
        found = pick(row, 32, jnp.dot(table[...], spot, preferred_element_type=f32), OWN_ROWS)
        held[c] = found

        @pl.when(jnp.logical_and(b < 3, up))
        def _():
            top_send[b] = jnp.concatenate([found[8 * k : 8 * k + 1] for k in range(4)], axis=0).astype(bf16)
            top_copy(b).start()

        return 0

    loads[5].wait()
    lax.fori_loop(0, 4, gather, 0)

    for load in loads[6:]:
        load.wait()

    for j in range(4):
        @pl.when(valid[j])
        def _():
            remote(gsend.at[j], grecv.at[j], g_s.at[j], g_r.at[j], g, p + OFFSETS[j]).wait_recv()

        @pl.when(jnp.logical_and(valid[j], down))
        def _():
            remote(lsend.at[j], lrecv.at[j], l_s.at[j], l_r.at[j], g, p + OFFSETS[j]).wait_recv()

    @pl.when(down)
    def _():
        low_copy.wait_recv()

    for i in range(2):
        late[i * 32 : (i + 1) * 32] = jnp.concatenate([grecv[2 * i], grecv[2 * i + 1]], axis=1)
    late8[0:64] = low_own[...]
    first = jnp.concatenate([lrecv[0], lrecv[1]], axis=1).astype(f32)[0:8]
    second = jnp.concatenate([lrecv[2], lrecv[3]], axis=1).astype(f32)[0:8]
    ghosts8 = first + pltpu.roll(second, 4, 0)
    late8[64:80] = jnp.concatenate([ghosts8, jnp.zeros((8, WIDE), f32)], axis=0).astype(bf16)

    row = rows[0:1, :]
    found = jnp.dot(late[...], hot[0], preferred_element_type=f32)
    held[0] = jnp.where(row == 17, found[32:64], jnp.where(row == 16, found[0:32], held[0]))
    both = pick(row >> 1, 8, jnp.dot(late8[...], hot[0], preferred_element_type=f32), ALL_ROWS // 2)
    low0[...] = jnp.where((row & 1) == 1, pltpu.roll(both, 4, 0), both)

    for i in range(3):
        @pl.when(down)
        def _():
            top_copy(i).wait_recv()

    def main_block(b, _):
        at = pl.ds(pl.multiple_of(b * MAIN_BLOCK, MAIN_BLOCK), MAIN_BLOCK)
        upper = [held[c, :, at] for c in range(4)]
        lowest = [low0[:, at]]
        for i in range(3):
            level = top_recv[i, :, at].astype(f32)
            lowest.append(jnp.concatenate([level, level], axis=0))
        term = element_terms(upper, lowest, stretch[:, at], shear[:, at], thick[:, at], rate[:, at])
        abuf[:, at] = jnp.sum(fac[:, at] * term, axis=0, keepdims=True)
        bbuf[:, at] = jnp.sum(off[:, at] * term, axis=0, keepdims=True)
        return 0

    lax.fori_loop(0, corners.shape[1] // MAIN_BLOCK, main_block, 0)

    from_all(en_send, en_recv, en_s, en_r)
    for i in range(layers):
        for k in range(per):
            at = slice((i * per + k) * WIDE, (i * per + k + 1) * WIDE)
            abuf[:, at] = 0.25 * (abuf[:, at] * en_recv[i, k : k + 1, :] + bbuf[:, at])

    def scatter(c, count):
        def block(b, total):
            at = slice(b * SCATTER_BLOCK, (b + 1) * SCATTER_BLOCK)
            line = iota((2 * count, SCATTER_BLOCK), 0)
            high, low = split_bf16(abuf[:, at])
            value = jnp.where(line < count, high, low)
            place = jnp.where(line < count, line, line - count)
            spread = jnp.where(place == rows[c : c + 1, at], value, 0.0).astype(bf16)
            return total + lax.dot_general(hot[c, :, at], spread, (((1,), (1,)), ((), ())), preferred_element_type=f32)

        total = block(0, jnp.zeros((WIDE, 2 * count), f32)).T
        return total[0:count] + total[count : 2 * count]

    core, chip, chips = lax.rem(g, 2), g // 2, layers // 2
    mate = g + 1 - 2 * core

    def ghost_sum(j, other):
        to = mate if other else g
        return remote(gh_send.at[j], gh_recv.at[core, 3 - j], gh_s.at[other, j], gh_r.at[core, 3 - j], to, p + OFFSETS[j])

    def ghost_from(j, k):
        return remote(gh_send.at[j], gh_recv.at[k, j], gh_s.at[0, j], gh_r.at[k, j], g, p + OFFSETS[j])

    nodes = scatter(0, 24)
    for j in range(4):
        gh_send[j] = nodes[OWN_ROWS + j // 2 : OWN_ROWS + j // 2 + 1, (j % 2) * 128 : (j % 2 + 1) * 128]
    for j in range(4):
        @pl.when(valid[j])
        def _():
            ghost_sum(j, 0).start()
            ghost_sum(j, 1).start()
    owned = nodes[0:OWN_ROWS]
    for c in range(1, 4):
        owned = owned + scatter(c, OWN_ROWS)
    owned = jnp.concatenate([owned[:, 0:128], owned[:, 128:256]], axis=0)

    pair_send[0] = owned[0:16]
    pair_send[1] = owned[16:32]
    pair = remote(pair_send.at[1 - core], pair_recv, pair_s, pair_r, mate, p)
    pair.start()

    line32 = iota((32, 512), 0)
    ids = jnp.concatenate([shared[d : d + 1, :] for d in range(4)], axis=1)
    hots = one_hot(ids & 127, 128)
    spots = (line32 & 15) + 16 * core == (ids >> 7)
    pair.wait_recv()
    for j in range(4):
        @pl.when(valid[j])
        def _():
            ghost_from(j, 0).wait_recv()
            ghost_from(j, 1).wait_recv()

    high, low = split_bf16(jnp.concatenate([gh_recv[0, d] + gh_recv[1, d] for d in range(4)], axis=1))
    spread = jnp.where(spots, jnp.where(line32 < 16, high, low), 0.0).astype(bf16)
    added = lax.dot_general(spread, hots, (((1,), (1,)), ((), ())), preferred_element_type=f32)
    all_recv[chip] = (pair_send[core] + pair_recv[...]) + (added[0:16] + added[16:32])

    def over_chips(k):
        i = lax.rem(chip + k, chips)
        return remote(all_recv.at[chip], all_recv.at[chip], all_s.at[i], all_r.at[chip], 2 * i + core, p)

    def from_chip(k):
        i = lax.rem(chip + k, chips)
        return remote(all_recv.at[chip], all_recv.at[i], all_s.at[i], all_r.at[i], 2 * i + core, p)

    def start_chip(k, _):
        over_chips(far_first(k, chips)).start()
        return 0

    def wait_chip(k, _):
        from_chip(k).wait_recv()
        return 0

    lax.fori_loop(0, chips - 1, start_chip, 0)
    sent_all(sc_send, sc_recv, sc_s, sc_r)
    sent_all(en_send, en_recv, en_s, en_r)
    pair.wait_send()
    for j in range(4):
        @pl.when(valid[j])
        def _():
            ghost(j).wait_send()
            ghost_sum(j, 0).wait_send()
            ghost_sum(j, 1).wait_send()

        @pl.when(jnp.logical_and(valid[j], up))
        def _():
            low_ghost(j).wait_send()

    @pl.when(up)
    def _():
        low_copy.wait_send()
        for i in range(3):
            top_copy(i).wait_send()

    lax.fori_loop(1, chips, wait_chip, 0)
    total = all_recv[0]
    for i in range(1, chips):
        total = total + all_recv[i]
    done[core] = total
    last = remote(done.at[core], done.at[core], last_s, last_r, mate, p)
    last.start()
    remote(done.at[core], done.at[1 - core], last_s, last_r, mate, p).wait_recv()
    out[0:16] = done[0]
    out[16:32] = done[1]

    def sent_chip(k, _):
        over_chips(k).wait_send()
        return 0

    lax.fori_loop(1, chips, sent_chip, 0)
    last.wait_send()


def shards(layers, planes, *args):
    velocity, adjoint, corners, shared, stretch, shear_part, thickness, rate_factor, retention, weight = args
    per = OWN_ROWS // layers
    elems = corners.shape[1]
    f32, bf16 = jnp.float32, jnp.bfloat16
    vmem, dma = pltpu.VMEM, pltpu.SemaphoreType.DMA
    args = [pltpu.with_memory_space_constraint(x, pltpu.HBM) for x in args]
    out = pl.pallas_call(
        functools.partial(kernel, layers, planes),
        out_shape=jax.ShapeDtypeStruct((32, 128), f32),
        in_specs=[pl.BlockSpec(memory_space=pltpu.HBM)] * 10,
        out_specs=pl.BlockSpec(memory_space=pltpu.VMEM),
        scratch_shapes=[vmem(a.shape, a.dtype) for a in args]
        + [
            vmem((OWN_ROWS * 32, WIDE), bf16), vmem((64, WIDE), bf16), vmem((80, WIDE), bf16),
            vmem((4, WIDE, elems), bf16), vmem((4, 32, elems), f32), vmem((4, elems), jnp.int32), vmem((8, elems), f32),
            vmem((3, 4, elems), bf16), vmem((3, 4, elems), bf16),
            vmem((64, WIDE), bf16), vmem((64, WIDE), bf16),
            vmem((4, 32, 128), bf16), vmem((4, 32, 128), bf16),
            vmem((4, 16, 128), bf16), vmem((4, 16, 128), bf16),
            vmem((8, elems), f32), vmem((8, elems), f32),
            vmem((layers, 2 * per, WIDE), f32), vmem((layers, 2 * per, WIDE), f32),
            vmem((layers, per, WIDE), f32), vmem((layers, per, WIDE), f32),
            vmem((1, elems), f32), vmem((1, elems), f32),
            vmem((4, 1, 128), f32), vmem((2, 4, 1, 128), f32),
            vmem((2, 16, 128), f32), vmem((16, 128), f32), vmem((layers // 2, 16, 128), f32), vmem((2, 16, 128), f32),
            dma((10,)), dma, dma, dma((3,)), dma((3,)), dma((4,)), dma((4,)), dma((4,)), dma((4,)),
        ]
        + [dma((layers,)), dma((layers,)), dma((layers,)), dma((layers,)), dma((2, 4)), dma((2, 4)), dma, dma]
        + [dma((layers // 2,)), dma((layers // 2,)), dma, dma],
        compiler_params=pltpu.CompilerParams(collective_id=0, has_side_effects=True, vmem_limit_bytes=40 << 20),
        name="ice_gradient",
    )(*args)
    return out.reshape(4096)


def solution(mesh):
    return jax.shard_map(
        functools.partial(shards, mesh.shape["layer"], mesh.shape["plane"]),
        mesh=mesh,
        in_specs=(
            P(None, "layer", "plane"),
            P(None, "layer", "plane"),
            P(None, "plane"),
            P(None, "plane"),
            P(None, "plane"),
            P(None, "plane"),
            P("layer", "plane"),
            P("layer", "plane"),
            P("layer", "plane"),
            P("layer", "plane"),
        ),
        out_specs=P("plane"),
        check_vma=False,
    )
```

```python
import functools
import math

import jax
import jax.numpy as jnp
from jax import lax
from jax.experimental import pallas as pl
from jax.experimental.pallas import tpu as pltpu
from jax.sharding import PartitionSpec as P

OFFSETS = (-2, -1, 1, 2)
STRAIN_EPS = 0.01
GAUSS = 1.0 / math.sqrt(3.0)
MESH = pl.DeviceIdType.MESH
WIDE = 256
HALF = 2048
OWN_ROWS = 16
ALL_ROWS = 18
MAIN_BLOCK = 512
SCATTER_BLOCK = 4096


def far_first(k, count):
    return count // 2 + (k + 1) // 2 * (2 * lax.rem(k, 2) - 1)


def iota(shape, axis):
    return lax.broadcasted_iota(jnp.int32, shape, axis)


def one_hot(low, width):
    return (iota((width, low.shape[1]), 0) == low).astype(jnp.float32).astype(jnp.bfloat16)


def place_of(ids):
    owned = ids < 2 * HALF
    row = jnp.where(owned, (ids >> 7) & 15, ids >> 8)
    spot = jnp.where(owned, (ids & 127) | ((ids >> 4) & 128), ids & 255)
    return row, spot


def owned_row(ref, lead, i):
    return jnp.concatenate([ref[lead, :, i * 128 : (i + 1) * 128], ref[lead, :, HALF + i * 128 : HALF + (i + 1) * 128]], axis=1)


def pick(row, size, table, count):
    out = table[0:size]
    for i in range(1, count):
        out = jnp.where(row == i, table[i * size : (i + 1) * size], out)
    return out


def corner_modes(v):
    p, q, r, s = v[1] - v[0], v[2] - v[3], v[0] + v[1], v[2] + v[3]
    return r + s, p + q, s - r, q - p


def element_terms(upper, lowest, stretch, shear, thick, rate):
    n = thick.shape[1]
    last = iota((8, n), 0) == 7
    top, end = corner_modes(upper), corner_modes(lowest)
    derived = []
    for comp in range(4):
        half, diff = [], []
        for m in range(4):
            t = top[m][comp * 8 : (comp + 1) * 8]
            b = jnp.where(last, pltpu.roll(end[m], 7 - comp, 0), pltpu.roll(t, 7, 0))
            d = t - b
            diff.append(d)
            if m:
                mean = t + b
                gd = GAUSS * d
                half.append((mean - gd, mean + gd))
        mx, my, mxy = half
        xi, eta = [], []
        for z in range(2):
            t = GAUSS * mxy[z]
            xi.append((mx[z] - t, mx[z] + t))
            eta.append((my[z] - t, my[z] + t))
        d0, dx, dy, dxy = diff
        gx, gy, gxy = GAUSS * dx, GAUSS * dy, (GAUSS * GAUSS) * dxy
        a0, a1, b0, b1 = d0 - gx, d0 + gx, gy - gxy, gy + gxy
        derived.append((xi, eta, ((a0 - b0, a0 + b0), (a1 - b1, a1 + b1))))
    s0, s1 = 0.125 * stretch[0:1], 0.125 * stretch[1:2]
    h0, h1 = 0.125 * shear[0:1], 0.125 * shear[1:2]
    inv = 0.125 / thick

    def strains(first, second):
        axi, aeta, az = derived[first]
        bxi, beta, bz = derived[second]
        two = range(2)
        return (
            [[s0 * axi[z][e] for e in two] for z in two],
            [[h0 * aeta[z][x] for x in two] for z in two],
            [[h1 * bxi[z][e] for e in two] for z in two],
            [[s1 * beta[z][x] for x in two] for z in two],
            [[h1 * axi[z][e] + s0 * bxi[z][e] for e in two] for z in two],
            [[s1 * aeta[z][x] + h0 * beta[z][x] for x in two] for z in two],
            [[inv * az[x][e] for e in two] for x in two],
            [[inv * bz[x][e] for e in two] for x in two],
        )

    f, g = strains(0, 1), strains(2, 3)
    total = None
    for x in range(2):
        for e in range(2):
            fxz, fyz, gxz, gyz = f[6][x][e], f[7][x][e], g[6][x][e], g[7][x][e]
            own_z = fxz * fxz + fyz * fyz + STRAIN_EPS
            cross_z = fxz * gxz + fyz * gyz
            for z in range(2):
                fxx, fyy = f[0][z][e] + f[1][z][x], f[2][z][e] + f[3][z][x]
                fxy = 0.5 * (f[4][z][e] + f[5][z][x])
                gxx, gyy = g[0][z][e] + g[1][z][x], g[2][z][e] + g[3][z][x]
                gxy = 0.5 * (g[4][z][e] + g[5][z][x])
                a, b = fxx + 0.5 * fyy, fyy + 0.5 * fxx
                effective = fxx * a + fyy * b + fxy * fxy + own_z
                cross = gxx * a + gyy * b + fxy * gxy + cross_z
                term = jnp.exp2((-1.0 / 3.0) * jnp.log2(effective)) * cross
                total = term if total is None else total + term
    det = stretch[0:1] * stretch[1:2] - shear[0:1] * shear[1:2]
    return (rate * thick) * (total / det)


def recurrence(keep, wei):
    sub = iota(keep.shape, 0)
    factor, offset = keep, (1.0 - keep) * wei
    for d in (1, 2, 4):
        before_f = jnp.where(sub >= d, pltpu.roll(factor, d, 0), 1.0)
        before_o = jnp.where(sub >= d, pltpu.roll(offset, d, 0), 0.0)
        offset = factor * before_o + offset
        factor = factor * before_f
    return factor, offset


def split_bf16(x):
    high = x.astype(jnp.bfloat16).astype(jnp.float32)
    return high, x - high


def kernel(
    layers,
    planes,
    vel_hbm, adj_hbm, cor_hbm, sha_hbm, str_hbm, she_hbm, thi_hbm, rat_hbm, ret_hbm, wei_hbm,
    out,
    vel, adj, corners, shared, stretch, shear, thick, rate, ret, wei,
    table, late, hot, held, rows, low0, top_send, top_recv, low_send, low_own, gsend, grecv, lsend, lrecv,
    fac, off, sc_send, sc_recv, en_send, en_recv,
    abuf, bbuf,
    gh_send, gh_recv, pair_send, pair_recv, all_recv, done,
    in_sem, low_s, low_r, top_s, top_r, g_s, g_r, l_s, l_r, sc_s, sc_r, en_s, en_r, gh_s, gh_r, pair_s, pair_r, all_s, all_r, last_s, last_r,
):
    g, p = lax.axis_index("layer"), lax.axis_index("plane")
    per = OWN_ROWS // layers
    f32, bf16 = jnp.float32, jnp.bfloat16

    hbm = (vel_hbm, adj_hbm, sha_hbm, ret_hbm, wei_hbm, cor_hbm, str_hbm, she_hbm, thi_hbm, rat_hbm)
    own = (vel, adj, shared, ret, wei, corners, stretch, shear, thick, rate)
    loads = [pltpu.make_async_copy(a, b, in_sem.at[i]) for i, (a, b) in enumerate(zip(hbm, own))]
    for load in loads:
        load.start()

    valid = [jnp.logical_and(p + o >= 0, p + o < planes) for o in OFFSETS]
    up, down = g > 0, g < layers - 1

    for d in range(4):
        @pl.when(jnp.logical_not(valid[d]))
        def _():
            grecv[d] = jnp.zeros(grecv.shape[1:], bf16)
            lrecv[d] = jnp.zeros(lrecv.shape[1:], bf16)
            gh_recv[0, d] = jnp.zeros(gh_recv.shape[2:], f32)
            gh_recv[1, d] = jnp.zeros(gh_recv.shape[2:], f32)

    @pl.when(jnp.logical_not(down))
    def _():
        low_own[...] = jnp.zeros(low_own.shape, bf16)
        lrecv[...] = jnp.zeros(lrecv.shape, bf16)
        top_recv[...] = jnp.zeros(top_recv.shape, bf16)

    barrier = pltpu.get_barrier_semaphore()

    def greet(layer, plane):
        pl.semaphore_signal(barrier, inc=1, device_id=(layer, plane), device_id_type=MESH)

    def greet_layer(r, _):
        greet(lax.rem(g + r, layers), p)
        return 0

    lax.fori_loop(1, layers, greet_layer, 0)
    expected = layers - 1
    for d, o in enumerate(OFFSETS):
        @pl.when(valid[d])
        def _():
            greet(g, p + o)

        @pl.when(jnp.logical_and(valid[d], up))
        def _():
            greet(g - 1, p + o)

        @pl.when(jnp.logical_and(valid[d], down))
        def _():
            greet(g + 1, p + o)

        expected = expected + valid[d].astype(jnp.int32) * (1 + up.astype(jnp.int32) + down.astype(jnp.int32))

    loads[0].wait()
    loads[1].wait()
    for i in range(OWN_ROWS):
        table[i * 32 : (i + 1) * 32] = jnp.concatenate([owned_row(f, k, i) for f in (vel, adj) for k in range(2)], axis=0)
    row8 = iota((8, WIDE), 0)
    pieces = []
    for i in range(0, OWN_ROWS, 2):
        piece = jnp.zeros((8, WIDE), f32)
        for half in range(2):
            for comp in range(4):
                level = owned_row((vel, adj)[comp // 2], comp % 2, i + half).astype(f32)
                piece = jnp.where(row8 == half * 4 + comp, level[0:1], piece)
        pieces.append(piece)
    low_send[...] = jnp.concatenate(pieces, axis=0).astype(bf16)
    loads[2].wait()
    row16 = iota((16, 128), 0)
    for j in range(4):
        ids = shared[j : j + 1, :]
        row, spot = place_of(ids)
        sent = jnp.dot(table[...], one_hot(spot, WIDE), preferred_element_type=f32)
        sent = pick(row, 32, sent, OWN_ROWS)
        gsend[j] = sent.astype(bf16)
        tops = jnp.zeros((16, 128), f32)
        for comp in range(4):
            tops = jnp.where(row16 == comp, sent[comp * 8 : comp * 8 + 1], tops)
        lsend[j] = tops.astype(bf16)
    loads[3].wait()
    loads[4].wait()
    for i in range(8):
        at = slice(i * 512, (i + 1) * 512)
        factor, offset = recurrence(ret[:, at], wei[:, at])
        fac[:, at] = factor
        off[:, at] = offset
    for i in range(layers):
        for k in range(per):
            at = slice((i * per + k) * WIDE, (i * per + k + 1) * WIDE)
            sc_send[i, k : k + 1, :] = fac[7:8, at]
            sc_send[i, per + k : per + k + 1, :] = off[7:8, at]

    pl.semaphore_wait(barrier, expected)

    def remote(src, dst, s, r, layer, plane):
        return pltpu.make_async_remote_copy(
            src_ref=src, dst_ref=dst, send_sem=s, recv_sem=r, device_id=(layer, plane), device_id_type=MESH
        )

    def to_all(send, recv, s, r):
        def copy(i):
            return remote(send.at[i], recv.at[g], s.at[i], r.at[g], i, p)

        def start(k, _):
            copy(lax.rem(g + far_first(k, layers), layers)).start()
            return 0

        lax.fori_loop(0, layers - 1, start, 0)

    def from_all(send, recv, s, r):
        def wait(k, _):
            i = lax.rem(g + k, layers)
            remote(send.at[i], recv.at[i], s.at[i], r.at[i], i, p).wait_recv()
            return 0

        lax.fori_loop(1, layers, wait, 0)

    def sent_all(send, recv, s, r):
        def wait(k, _):
            i = lax.rem(g + k, layers)
            remote(send.at[i], recv.at[i], s.at[i], r.at[i], i, p).wait_send()
            return 0

        lax.fori_loop(1, layers, wait, 0)

    def ghost(j):
        return remote(gsend.at[j], grecv.at[3 - j], g_s.at[j], g_r.at[3 - j], g, p + OFFSETS[j])

    def low_ghost(j):
        return remote(lsend.at[j], lrecv.at[3 - j], l_s.at[j], l_r.at[3 - j], g - 1, p + OFFSETS[j])

    low_copy = remote(low_send, low_own, low_s, low_r, g - 1, p)

    to_all(sc_send, sc_recv, sc_s, sc_r)

    for j in range(4):
        @pl.when(valid[j])
        def _():
            ghost(j).start()

        @pl.when(jnp.logical_and(valid[j], up))
        def _():
            low_ghost(j).start()

    @pl.when(up)
    def _():
        low_copy.start()

    def top_copy(i):
        return remote(top_send.at[i], top_recv.at[i], top_s.at[i], top_r.at[i], g - 1, p)

    def enter():
        sc_recv[g] = sc_send[g]
        from_all(sc_send, sc_recv, sc_s, sc_r)
        running = jnp.zeros((per, WIDE), f32)
        for i in range(layers):
            en_send[i] = running
            running = sc_recv[i, 0:per, :] * running + sc_recv[i, per : 2 * per, :]
        to_all(en_send, en_recv, en_s, en_r)
        en_recv[g] = en_send[g]

    def gather(b, _):
        @pl.when(b == 3)
        def _():
            enter()

        c = lax.rem(b + 1, 4)
        row, spot = place_of(corners[pl.ds(c, 1), :])
        spot = one_hot(spot, WIDE)
        rows[pl.ds(c, 1), :] = row
        hot[c] = spot
        found = pick(row, 32, jnp.dot(table[...], spot, preferred_element_type=f32), OWN_ROWS)
        held[c] = found

        @pl.when(jnp.logical_and(b < 3, up))
        def _():
            top_send[b] = jnp.concatenate([found[8 * k : 8 * k + 1] for k in range(4)], axis=0).astype(bf16)
            top_copy(b).start()

        return 0

    loads[5].wait()
    lax.fori_loop(0, 4, gather, 0)

    for load in loads[6:]:
        load.wait()

    for j in range(4):
        @pl.when(valid[j])
        def _():
            remote(gsend.at[j], grecv.at[j], g_s.at[j], g_r.at[j], g, p + OFFSETS[j]).wait_recv()

        @pl.when(jnp.logical_and(valid[j], down))
        def _():
            remote(lsend.at[j], lrecv.at[j], l_s.at[j], l_r.at[j], g, p + OFFSETS[j]).wait_recv()

    @pl.when(down)
    def _():
        low_copy.wait_recv()

    for i in range(2):
        late[i * 32 : (i + 1) * 32] = jnp.concatenate([grecv[2 * i], grecv[2 * i + 1]], axis=1)
    late[64:128] = low_own[...]
    first = jnp.concatenate([lrecv[0], lrecv[1]], axis=1).astype(f32)[0:8]
    second = jnp.concatenate([lrecv[2], lrecv[3]], axis=1).astype(f32)[0:8]
    ghosts8 = first + pltpu.roll(second, 4, 0)
    late[128:144] = jnp.concatenate([ghosts8, jnp.zeros((8, WIDE), f32)], axis=0).astype(bf16)

    row = rows[0:1, :]
    found = jnp.dot(late[...], hot[0], preferred_element_type=f32)
    held[0] = jnp.where(row == 17, found[32:64], jnp.where(row == 16, found[0:32], held[0]))
    both = pick(row >> 1, 8, found[64:136], ALL_ROWS // 2)
    low0[...] = jnp.where((row & 1) == 1, pltpu.roll(both, 4, 0), both)

    for i in range(3):
        @pl.when(down)
        def _():
            top_copy(i).wait_recv()

    def main_block(b, _):
        at = pl.ds(pl.multiple_of(b * MAIN_BLOCK, MAIN_BLOCK), MAIN_BLOCK)
        upper = [held[c, :, at] for c in range(4)]
        lowest = [low0[:, at]]
        for i in range(3):
            level = top_recv[i, :, at].astype(f32)
            lowest.append(jnp.concatenate([level, level], axis=0))
        term = element_terms(upper, lowest, stretch[:, at], shear[:, at], thick[:, at], rate[:, at])
        abuf[:, at] = jnp.sum(fac[:, at] * term, axis=0, keepdims=True)
        bbuf[:, at] = jnp.sum(off[:, at] * term, axis=0, keepdims=True)
        return 0

    lax.fori_loop(0, corners.shape[1] // MAIN_BLOCK, main_block, 0)

    from_all(en_send, en_recv, en_s, en_r)
    for i in range(layers):
        for k in range(per):
            at = slice((i * per + k) * WIDE, (i * per + k + 1) * WIDE)
            abuf[:, at] = 0.25 * (abuf[:, at] * en_recv[i, k : k + 1, :] + bbuf[:, at])

    def scatter(c, count):
        def block(b, total):
            at = slice(b * SCATTER_BLOCK, (b + 1) * SCATTER_BLOCK)
            line = iota((2 * count, SCATTER_BLOCK), 0)
            high, low = split_bf16(abuf[:, at])
            value = jnp.where(line < count, high, low)
            place = jnp.where(line < count, line, line - count)
            spread = jnp.where(place == rows[c : c + 1, at], value, 0.0).astype(bf16)
            return total + lax.dot_general(hot[c, :, at], spread, (((1,), (1,)), ((), ())), preferred_element_type=f32)

        total = block(0, jnp.zeros((WIDE, 2 * count), f32)).T
        return total[0:count] + total[count : 2 * count]

    core, chip, chips = lax.rem(g, 2), g // 2, layers // 2
    mate = g + 1 - 2 * core

    def ghost_sum(j, other):
        to = mate if other else g
        return remote(gh_send.at[j], gh_recv.at[core, 3 - j], gh_s.at[other, j], gh_r.at[core, 3 - j], to, p + OFFSETS[j])

    def ghost_from(j, k):
        return remote(gh_send.at[j], gh_recv.at[k, j], gh_s.at[0, j], gh_r.at[k, j], g, p + OFFSETS[j])

    nodes = scatter(0, 24)
    for j in range(4):
        gh_send[j] = nodes[OWN_ROWS + j // 2 : OWN_ROWS + j // 2 + 1, (j % 2) * 128 : (j % 2 + 1) * 128]
    for j in range(4):
        @pl.when(valid[j])
        def _():
            ghost_sum(j, 0).start()
            ghost_sum(j, 1).start()
    owned = nodes[0:OWN_ROWS]
    for c in range(1, 4):
        owned = owned + scatter(c, OWN_ROWS)
    owned = jnp.concatenate([owned[:, 0:128], owned[:, 128:256]], axis=0)

    pair_send[0] = owned[0:16]
    pair_send[1] = owned[16:32]
    pair = remote(pair_send.at[1 - core], pair_recv, pair_s, pair_r, mate, p)
    pair.start()

    line32 = iota((32, 512), 0)
    ids = jnp.concatenate([shared[d : d + 1, :] for d in range(4)], axis=1)
    hots = one_hot(ids & 127, 128)
    spots = (line32 & 15) + 16 * core == (ids >> 7)
    pair.wait_recv()
    for j in range(4):
        @pl.when(valid[j])
        def _():
            ghost_from(j, 0).wait_recv()
            ghost_from(j, 1).wait_recv()

    high, low = split_bf16(jnp.concatenate([gh_recv[0, d] + gh_recv[1, d] for d in range(4)], axis=1))
    spread = jnp.where(spots, jnp.where(line32 < 16, high, low), 0.0).astype(bf16)
    added = lax.dot_general(spread, hots, (((1,), (1,)), ((), ())), preferred_element_type=f32)
    all_recv[chip] = (pair_send[core] + pair_recv[...]) + (added[0:16] + added[16:32])

    def over_chips(k):
        i = lax.rem(chip + k, chips)
        return remote(all_recv.at[chip], all_recv.at[chip], all_s.at[i], all_r.at[chip], 2 * i + core, p)

    def from_chip(k):
        i = lax.rem(chip + k, chips)
        return remote(all_recv.at[chip], all_recv.at[i], all_s.at[i], all_r.at[i], 2 * i + core, p)

    def start_chip(k, _):
        over_chips(far_first(k, chips)).start()
        return 0

    def wait_chip(k, _):
        from_chip(k).wait_recv()
        return 0

    lax.fori_loop(0, chips - 1, start_chip, 0)
    sent_all(sc_send, sc_recv, sc_s, sc_r)
    sent_all(en_send, en_recv, en_s, en_r)
    pair.wait_send()
    for j in range(4):
        @pl.when(valid[j])
        def _():
            ghost(j).wait_send()
            ghost_sum(j, 0).wait_send()
            ghost_sum(j, 1).wait_send()

        @pl.when(jnp.logical_and(valid[j], up))
        def _():
            low_ghost(j).wait_send()

    @pl.when(up)
    def _():
        low_copy.wait_send()
        for i in range(3):
            top_copy(i).wait_send()

    lax.fori_loop(1, chips, wait_chip, 0)
    total = all_recv[0]
    for i in range(1, chips):
        total = total + all_recv[i]
    done[core] = total
    last = remote(done.at[core], done.at[core], last_s, last_r, mate, p)
    last.start()
    remote(done.at[core], done.at[1 - core], last_s, last_r, mate, p).wait_recv()
    out[0:16] = done[0]
    out[16:32] = done[1]

    def sent_chip(k, _):
        over_chips(k).wait_send()
        return 0

    lax.fori_loop(1, chips, sent_chip, 0)
    last.wait_send()


def shards(layers, planes, *args):
    velocity, adjoint, corners, shared, stretch, shear_part, thickness, rate_factor, retention, weight = args
    per = OWN_ROWS // layers
    elems = corners.shape[1]
    f32, bf16 = jnp.float32, jnp.bfloat16
    vmem, dma = pltpu.VMEM, pltpu.SemaphoreType.DMA
    args = [pltpu.with_memory_space_constraint(x, pltpu.HBM) for x in args]
    out = pl.pallas_call(
        functools.partial(kernel, layers, planes),
        out_shape=jax.ShapeDtypeStruct((32, 128), f32),
        in_specs=[pl.BlockSpec(memory_space=pltpu.HBM)] * 10,
        out_specs=pl.BlockSpec(memory_space=pltpu.VMEM),
        scratch_shapes=[vmem(a.shape, a.dtype) for a in args]
        + [
            vmem((OWN_ROWS * 32, WIDE), bf16), vmem((144, WIDE), bf16),
            vmem((4, WIDE, elems), bf16), vmem((4, 32, elems), f32), vmem((4, elems), jnp.int32), vmem((8, elems), f32),
            vmem((3, 4, elems), bf16), vmem((3, 4, elems), bf16),
            vmem((64, WIDE), bf16), vmem((64, WIDE), bf16),
            vmem((4, 32, 128), bf16), vmem((4, 32, 128), bf16),
            vmem((4, 16, 128), bf16), vmem((4, 16, 128), bf16),
            vmem((8, elems), f32), vmem((8, elems), f32),
            vmem((layers, 2 * per, WIDE), f32), vmem((layers, 2 * per, WIDE), f32),
            vmem((layers, per, WIDE), f32), vmem((layers, per, WIDE), f32),
            vmem((1, elems), f32), vmem((1, elems), f32),
            vmem((4, 1, 128), f32), vmem((2, 4, 1, 128), f32),
            vmem((2, 16, 128), f32), vmem((16, 128), f32), vmem((layers // 2, 16, 128), f32), vmem((2, 16, 128), f32),
            dma((10,)), dma, dma, dma((3,)), dma((3,)), dma((4,)), dma((4,)), dma((4,)), dma((4,)),
        ]
        + [dma((layers,)), dma((layers,)), dma((layers,)), dma((layers,)), dma((2, 4)), dma((2, 4)), dma, dma]
        + [dma((layers // 2,)), dma((layers // 2,)), dma, dma],
        compiler_params=pltpu.CompilerParams(collective_id=0, has_side_effects=True, vmem_limit_bytes=40 << 20),
        name="ice_gradient",
    )(*args)
    return out.reshape(4096)


def solution(mesh):
    return jax.shard_map(
        functools.partial(shards, mesh.shape["layer"], mesh.shape["plane"]),
        mesh=mesh,
        in_specs=(
            P(None, "layer", "plane"),
            P(None, "layer", "plane"),
            P(None, "plane"),
            P(None, "plane"),
            P(None, "plane"),
            P(None, "plane"),
            P("layer", "plane"),
            P("layer", "plane"),
            P("layer", "plane"),
            P("layer", "plane"),
        ),
        out_specs=P("plane"),
        check_vma=False,
    )
```

```python
import functools
import math

import jax
import jax.numpy as jnp
from jax import lax
from jax.experimental import pallas as pl
from jax.experimental.pallas import tpu as pltpu
from jax.sharding import PartitionSpec as P

OFFSETS = (-2, -1, 1, 2)
STRAIN_EPS = 0.01
GAUSS = 1.0 / math.sqrt(3.0)
MESH = pl.DeviceIdType.MESH
WIDE = 256
HALF = 2048
OWN_ROWS = 16
ALL_ROWS = 18
MAIN_BLOCK = 256
SCATTER_BLOCK = 4096


def far_first(k, count):
    return count // 2 + (k + 1) // 2 * (2 * lax.rem(k, 2) - 1)


def iota(shape, axis):
    return lax.broadcasted_iota(jnp.int32, shape, axis)


def one_hot(low, width):
    return (iota((width, low.shape[1]), 0) == low).astype(jnp.float32).astype(jnp.bfloat16)


def place_of(ids):
    owned = ids < 2 * HALF
    row = jnp.where(owned, (ids >> 7) & 15, ids >> 8)
    spot = jnp.where(owned, (ids & 127) | ((ids >> 4) & 128), ids & 255)
    return row, spot


def owned_row(ref, lead, i):
    return jnp.concatenate([ref[lead, :, i * 128 : (i + 1) * 128], ref[lead, :, HALF + i * 128 : HALF + (i + 1) * 128]], axis=1)


def pick(row, size, table, count):
    out = table[0:size]
    for i in range(1, count):
        out = jnp.where(row == i, table[i * size : (i + 1) * size], out)
    return out


def corner_modes(v):
    p, q, r, s = v[1] - v[0], v[2] - v[3], v[0] + v[1], v[2] + v[3]
    return r + s, p + q, s - r, q - p


def element_terms(upper, lowest, stretch, shear, thick, rate):
    n = thick.shape[1]
    last = iota((8, n), 0) == 7
    top, end = corner_modes(upper), corner_modes(lowest)
    derived = []
    for comp in range(4):
        half, diff = [], []
        for m in range(4):
            t = top[m][comp * 8 : (comp + 1) * 8]
            b = jnp.where(last, pltpu.roll(end[m], 7 - comp, 0), pltpu.roll(t, 7, 0))
            d = t - b
            diff.append(d)
            if m:
                mean = t + b
                gd = GAUSS * d
                half.append((mean - gd, mean + gd))
        mx, my, mxy = half
        xi, eta = [], []
        for z in range(2):
            t = GAUSS * mxy[z]
            xi.append((mx[z] - t, mx[z] + t))
            eta.append((my[z] - t, my[z] + t))
        d0, dx, dy, dxy = diff
        gx, gy, gxy = GAUSS * dx, GAUSS * dy, (GAUSS * GAUSS) * dxy
        a0, a1, b0, b1 = d0 - gx, d0 + gx, gy - gxy, gy + gxy
        derived.append((xi, eta, ((a0 - b0, a0 + b0), (a1 - b1, a1 + b1))))
    s0, s1 = 0.125 * stretch[0:1], 0.125 * stretch[1:2]
    h0, h1 = 0.125 * shear[0:1], 0.125 * shear[1:2]
    inv = 0.125 / thick

    def strains(first, second):
        axi, aeta, az = derived[first]
        bxi, beta, bz = derived[second]
        two = range(2)
        return (
            [[s0 * axi[z][e] for e in two] for z in two],
            [[h0 * aeta[z][x] for x in two] for z in two],
            [[h1 * bxi[z][e] for e in two] for z in two],
            [[s1 * beta[z][x] for x in two] for z in two],
            [[h1 * axi[z][e] + s0 * bxi[z][e] for e in two] for z in two],
            [[s1 * aeta[z][x] + h0 * beta[z][x] for x in two] for z in two],
            [[inv * az[x][e] for e in two] for x in two],
            [[inv * bz[x][e] for e in two] for x in two],
        )

    f, g = strains(0, 1), strains(2, 3)
    total = None
    for x in range(2):
        for e in range(2):
            fxz, fyz, gxz, gyz = f[6][x][e], f[7][x][e], g[6][x][e], g[7][x][e]
            own_z = fxz * fxz + fyz * fyz + STRAIN_EPS
            cross_z = fxz * gxz + fyz * gyz
            for z in range(2):
                fxx, fyy = f[0][z][e] + f[1][z][x], f[2][z][e] + f[3][z][x]
                fxy = 0.5 * (f[4][z][e] + f[5][z][x])
                gxx, gyy = g[0][z][e] + g[1][z][x], g[2][z][e] + g[3][z][x]
                gxy = 0.5 * (g[4][z][e] + g[5][z][x])
                a, b = fxx + 0.5 * fyy, fyy + 0.5 * fxx
                effective = fxx * a + fyy * b + fxy * fxy + own_z
                cross = gxx * a + gyy * b + fxy * gxy + cross_z
                term = jnp.exp2((-1.0 / 3.0) * jnp.log2(effective)) * cross
                total = term if total is None else total + term
    det = stretch[0:1] * stretch[1:2] - shear[0:1] * shear[1:2]
    return (rate * thick) * (total / det)


def recurrence(keep, wei):
    sub = iota(keep.shape, 0)
    factor, offset = keep, (1.0 - keep) * wei
    for d in (1, 2, 4):
        before_f = jnp.where(sub >= d, pltpu.roll(factor, d, 0), 1.0)
        before_o = jnp.where(sub >= d, pltpu.roll(offset, d, 0), 0.0)
        offset = factor * before_o + offset
        factor = factor * before_f
    return factor, offset


def split_bf16(x):
    high = x.astype(jnp.bfloat16).astype(jnp.float32)
    return high, x - high


def kernel(
    layers,
    planes,
    vel_hbm, adj_hbm, cor_hbm, sha_hbm, str_hbm, she_hbm, thi_hbm, rat_hbm, ret_hbm, wei_hbm,
    out,
    vel, adj, corners, shared, stretch, shear, thick, rate, ret, wei,
    table, late, hot, held, rows, low0, top_send, top_recv, low_send, low_own, gsend, grecv, lsend, lrecv,
    fac, off, sc_send, sc_recv, en_send, en_recv,
    abuf, bbuf,
    gh_send, gh_recv, pair_send, pair_recv, all_recv, done,
    in_sem, low_s, low_r, top_s, top_r, g_s, g_r, l_s, l_r, sc_s, sc_r, en_s, en_r, gh_s, gh_r, pair_s, pair_r, all_s, all_r, last_s, last_r,
):
    g, p = lax.axis_index("layer"), lax.axis_index("plane")
    per = OWN_ROWS // layers
    f32, bf16 = jnp.float32, jnp.bfloat16

    hbm = (vel_hbm, adj_hbm, sha_hbm, ret_hbm, wei_hbm, cor_hbm, str_hbm, she_hbm, thi_hbm, rat_hbm)
    own = (vel, adj, shared, ret, wei, corners, stretch, shear, thick, rate)
    loads = [pltpu.make_async_copy(a, b, in_sem.at[i]) for i, (a, b) in enumerate(zip(hbm, own))]
    for load in loads:
        load.start()

    valid = [jnp.logical_and(p + o >= 0, p + o < planes) for o in OFFSETS]
    up, down = g > 0, g < layers - 1

    for d in range(4):
        @pl.when(jnp.logical_not(valid[d]))
        def _():
            grecv[d] = jnp.zeros(grecv.shape[1:], bf16)
            lrecv[d] = jnp.zeros(lrecv.shape[1:], bf16)
            gh_recv[0, d] = jnp.zeros(gh_recv.shape[2:], f32)
            gh_recv[1, d] = jnp.zeros(gh_recv.shape[2:], f32)

    @pl.when(jnp.logical_not(down))
    def _():
        low_own[...] = jnp.zeros(low_own.shape, bf16)
        lrecv[...] = jnp.zeros(lrecv.shape, bf16)
        top_recv[...] = jnp.zeros(top_recv.shape, bf16)

    barrier = pltpu.get_barrier_semaphore()

    def greet(layer, plane):
        pl.semaphore_signal(barrier, inc=1, device_id=(layer, plane), device_id_type=MESH)

    def greet_layer(r, _):
        greet(lax.rem(g + r, layers), p)
        return 0

    lax.fori_loop(1, layers, greet_layer, 0)
    expected = layers - 1
    for d, o in enumerate(OFFSETS):
        @pl.when(valid[d])
        def _():
            greet(g, p + o)

        @pl.when(jnp.logical_and(valid[d], up))
        def _():
            greet(g - 1, p + o)

        @pl.when(jnp.logical_and(valid[d], down))
        def _():
            greet(g + 1, p + o)

        expected = expected + valid[d].astype(jnp.int32) * (1 + up.astype(jnp.int32) + down.astype(jnp.int32))

    loads[0].wait()
    loads[1].wait()
    for i in range(OWN_ROWS):
        table[i * 32 : (i + 1) * 32] = jnp.concatenate([owned_row(f, k, i) for f in (vel, adj) for k in range(2)], axis=0)
    row8 = iota((8, WIDE), 0)
    pieces = []
    for i in range(0, OWN_ROWS, 2):
        piece = jnp.zeros((8, WIDE), f32)
        for half in range(2):
            for comp in range(4):
                level = owned_row((vel, adj)[comp // 2], comp % 2, i + half).astype(f32)
                piece = jnp.where(row8 == half * 4 + comp, level[0:1], piece)
        pieces.append(piece)
    low_send[...] = jnp.concatenate(pieces, axis=0).astype(bf16)
    loads[2].wait()
    row16 = iota((16, 128), 0)
    for j in range(4):
        ids = shared[j : j + 1, :]
        row, spot = place_of(ids)
        sent = jnp.dot(table[...], one_hot(spot, WIDE), preferred_element_type=f32)
        sent = pick(row, 32, sent, OWN_ROWS)
        gsend[j] = sent.astype(bf16)
        tops = jnp.zeros((16, 128), f32)
        for comp in range(4):
            tops = jnp.where(row16 == comp, sent[comp * 8 : comp * 8 + 1], tops)
        lsend[j] = tops.astype(bf16)
    loads[3].wait()
    loads[4].wait()
    for i in range(8):
        at = slice(i * 512, (i + 1) * 512)
        factor, offset = recurrence(ret[:, at], wei[:, at])
        fac[:, at] = factor
        off[:, at] = offset
    for i in range(layers):
        for k in range(per):
            at = slice((i * per + k) * WIDE, (i * per + k + 1) * WIDE)
            sc_send[i, k : k + 1, :] = fac[7:8, at]
            sc_send[i, per + k : per + k + 1, :] = off[7:8, at]

    pl.semaphore_wait(barrier, expected)

    def remote(src, dst, s, r, layer, plane):
        return pltpu.make_async_remote_copy(
            src_ref=src, dst_ref=dst, send_sem=s, recv_sem=r, device_id=(layer, plane), device_id_type=MESH
        )

    def to_all(send, recv, s, r):
        def copy(i):
            return remote(send.at[i], recv.at[g], s.at[i], r.at[g], i, p)

        def start(k, _):
            copy(lax.rem(g + far_first(k, layers), layers)).start()
            return 0

        lax.fori_loop(0, layers - 1, start, 0)

    def from_all(send, recv, s, r):
        def wait(k, _):
            i = lax.rem(g + k, layers)
            remote(send.at[i], recv.at[i], s.at[i], r.at[i], i, p).wait_recv()
            return 0

        lax.fori_loop(1, layers, wait, 0)

    def sent_all(send, recv, s, r):
        def wait(k, _):
            i = lax.rem(g + k, layers)
            remote(send.at[i], recv.at[i], s.at[i], r.at[i], i, p).wait_send()
            return 0

        lax.fori_loop(1, layers, wait, 0)

    def ghost(j):
        return remote(gsend.at[j], grecv.at[3 - j], g_s.at[j], g_r.at[3 - j], g, p + OFFSETS[j])

    def low_ghost(j):
        return remote(lsend.at[j], lrecv.at[3 - j], l_s.at[j], l_r.at[3 - j], g - 1, p + OFFSETS[j])

    low_copy = remote(low_send, low_own, low_s, low_r, g - 1, p)

    to_all(sc_send, sc_recv, sc_s, sc_r)

    for j in range(4):
        @pl.when(valid[j])
        def _():
            ghost(j).start()

        @pl.when(jnp.logical_and(valid[j], up))
        def _():
            low_ghost(j).start()

    @pl.when(up)
    def _():
        low_copy.start()

    def top_copy(i):
        return remote(top_send.at[i], top_recv.at[i], top_s.at[i], top_r.at[i], g - 1, p)

    def enter():
        sc_recv[g] = sc_send[g]
        from_all(sc_send, sc_recv, sc_s, sc_r)
        running = jnp.zeros((per, WIDE), f32)
        for i in range(layers):
            en_send[i] = running
            running = sc_recv[i, 0:per, :] * running + sc_recv[i, per : 2 * per, :]
        to_all(en_send, en_recv, en_s, en_r)
        en_recv[g] = en_send[g]

    def gather(b, _):
        @pl.when(b == 3)
        def _():
            enter()

        c = lax.rem(b + 1, 4)
        row, spot = place_of(corners[pl.ds(c, 1), :])
        spot = one_hot(spot, WIDE)
        rows[pl.ds(c, 1), :] = row
        hot[c] = spot
        found = pick(row, 32, jnp.dot(table[...], spot, preferred_element_type=f32), OWN_ROWS)
        held[c] = found

        @pl.when(jnp.logical_and(b < 3, up))
        def _():
            top_send[b] = jnp.concatenate([found[8 * k : 8 * k + 1] for k in range(4)], axis=0).astype(bf16)
            top_copy(b).start()

        return 0

    loads[5].wait()
    lax.fori_loop(0, 4, gather, 0)

    for load in loads[6:]:
        load.wait()

    for j in range(4):
        @pl.when(valid[j])
        def _():
            remote(gsend.at[j], grecv.at[j], g_s.at[j], g_r.at[j], g, p + OFFSETS[j]).wait_recv()

        @pl.when(jnp.logical_and(valid[j], down))
        def _():
            remote(lsend.at[j], lrecv.at[j], l_s.at[j], l_r.at[j], g, p + OFFSETS[j]).wait_recv()

    @pl.when(down)
    def _():
        low_copy.wait_recv()

    for i in range(2):
        late[i * 32 : (i + 1) * 32] = jnp.concatenate([grecv[2 * i], grecv[2 * i + 1]], axis=1)
    late[64:128] = low_own[...]
    first = jnp.concatenate([lrecv[0], lrecv[1]], axis=1).astype(f32)[0:8]
    second = jnp.concatenate([lrecv[2], lrecv[3]], axis=1).astype(f32)[0:8]
    ghosts8 = first + pltpu.roll(second, 4, 0)
    late[128:144] = jnp.concatenate([ghosts8, jnp.zeros((8, WIDE), f32)], axis=0).astype(bf16)

    row = rows[0:1, :]
    found = jnp.dot(late[...], hot[0], preferred_element_type=f32)
    held[0] = jnp.where(row == 17, found[32:64], jnp.where(row == 16, found[0:32], held[0]))
    both = pick(row >> 1, 8, found[64:136], ALL_ROWS // 2)
    low0[...] = jnp.where((row & 1) == 1, pltpu.roll(both, 4, 0), both)

    for i in range(3):
        @pl.when(down)
        def _():
            top_copy(i).wait_recv()

    def main_block(b, _):
        at = pl.ds(pl.multiple_of(b * MAIN_BLOCK, MAIN_BLOCK), MAIN_BLOCK)
        upper = [held[c, :, at] for c in range(4)]
        lowest = [low0[:, at]]
        for i in range(3):
            level = top_recv[i, :, at].astype(f32)
            lowest.append(jnp.concatenate([level, level], axis=0))
        term = element_terms(upper, lowest, stretch[:, at], shear[:, at], thick[:, at], rate[:, at])
        abuf[:, at] = jnp.sum(fac[:, at] * term, axis=0, keepdims=True)
        bbuf[:, at] = jnp.sum(off[:, at] * term, axis=0, keepdims=True)
        return 0

    lax.fori_loop(0, corners.shape[1] // MAIN_BLOCK, main_block, 0)

    from_all(en_send, en_recv, en_s, en_r)
    for i in range(layers):
        for k in range(per):
            at = slice((i * per + k) * WIDE, (i * per + k + 1) * WIDE)
            abuf[:, at] = 0.25 * (abuf[:, at] * en_recv[i, k : k + 1, :] + bbuf[:, at])

    def scatter(which, count):
        def block(b, c, total):
            at = slice(b * SCATTER_BLOCK, (b + 1) * SCATTER_BLOCK)
            line = iota((2 * count, SCATTER_BLOCK), 0)
            high, low = split_bf16(abuf[:, at])
            value = jnp.where(line < count, high, low)
            place = jnp.where(line < count, line, line - count)
            spread = jnp.where(place == rows[c : c + 1, at], value, 0.0).astype(bf16)
            return total + lax.dot_general(hot[c, :, at], spread, (((1,), (1,)), ((), ())), preferred_element_type=f32)

        total = jnp.zeros((WIDE, 2 * count), f32)
        for c in which:
            total = block(0, c, total)
        total = total.T
        return total[0:count] + total[count : 2 * count]

    core, chip, chips = lax.rem(g, 2), g // 2, layers // 2
    mate = g + 1 - 2 * core

    def ghost_sum(j, other):
        to = mate if other else g
        return remote(gh_send.at[j], gh_recv.at[core, 3 - j], gh_s.at[other, j], gh_r.at[core, 3 - j], to, p + OFFSETS[j])

    def ghost_from(j, k):
        return remote(gh_send.at[j], gh_recv.at[k, j], gh_s.at[0, j], gh_r.at[k, j], g, p + OFFSETS[j])

    nodes = scatter((0,), 24)
    for j in range(4):
        gh_send[j] = nodes[OWN_ROWS + j // 2 : OWN_ROWS + j // 2 + 1, (j % 2) * 128 : (j % 2 + 1) * 128]
    for j in range(4):
        @pl.when(valid[j])
        def _():
            ghost_sum(j, 0).start()
            ghost_sum(j, 1).start()
    owned = nodes[0:OWN_ROWS] + scatter((1, 2, 3), OWN_ROWS)
    owned = jnp.concatenate([owned[:, 0:128], owned[:, 128:256]], axis=0)

    pair_send[0] = owned[0:16]
    pair_send[1] = owned[16:32]
    pair = remote(pair_send.at[1 - core], pair_recv, pair_s, pair_r, mate, p)
    pair.start()

    line32 = iota((32, 512), 0)
    ids = jnp.concatenate([shared[d : d + 1, :] for d in range(4)], axis=1)
    hots = one_hot(ids & 127, 128)
    spots = (line32 & 15) + 16 * core == (ids >> 7)
    pair.wait_recv()
    for j in range(4):
        @pl.when(valid[j])
        def _():
            ghost_from(j, 0).wait_recv()
            ghost_from(j, 1).wait_recv()

    high, low = split_bf16(jnp.concatenate([gh_recv[0, d] + gh_recv[1, d] for d in range(4)], axis=1))
    spread = jnp.where(spots, jnp.where(line32 < 16, high, low), 0.0).astype(bf16)
    added = lax.dot_general(spread, hots, (((1,), (1,)), ((), ())), preferred_element_type=f32)
    all_recv[chip] = (pair_send[core] + pair_recv[...]) + (added[0:16] + added[16:32])

    def over_chips(k):
        i = lax.rem(chip + k, chips)
        return remote(all_recv.at[chip], all_recv.at[chip], all_s.at[i], all_r.at[chip], 2 * i + core, p)

    def from_chip(k):
        i = lax.rem(chip + k, chips)
        return remote(all_recv.at[chip], all_recv.at[i], all_s.at[i], all_r.at[i], 2 * i + core, p)

    def start_chip(k, _):
        over_chips(far_first(k, chips)).start()
        return 0

    def wait_chip(k, _):
        from_chip(k).wait_recv()
        return 0

    lax.fori_loop(0, chips - 1, start_chip, 0)
    sent_all(sc_send, sc_recv, sc_s, sc_r)
    sent_all(en_send, en_recv, en_s, en_r)
    pair.wait_send()
    for j in range(4):
        @pl.when(valid[j])
        def _():
            ghost(j).wait_send()
            ghost_sum(j, 0).wait_send()
            ghost_sum(j, 1).wait_send()

        @pl.when(jnp.logical_and(valid[j], up))
        def _():
            low_ghost(j).wait_send()

    @pl.when(up)
    def _():
        low_copy.wait_send()
        for i in range(3):
            top_copy(i).wait_send()

    lax.fori_loop(1, chips, wait_chip, 0)
    total = all_recv[0]
    for i in range(1, chips):
        total = total + all_recv[i]
    done[core] = total
    last = remote(done.at[core], done.at[core], last_s, last_r, mate, p)
    last.start()
    remote(done.at[core], done.at[1 - core], last_s, last_r, mate, p).wait_recv()
    out[0:16] = done[0]
    out[16:32] = done[1]

    def sent_chip(k, _):
        over_chips(k).wait_send()
        return 0

    lax.fori_loop(1, chips, sent_chip, 0)
    last.wait_send()


def shards(layers, planes, *args):
    velocity, adjoint, corners, shared, stretch, shear_part, thickness, rate_factor, retention, weight = args
    per = OWN_ROWS // layers
    elems = corners.shape[1]
    f32, bf16 = jnp.float32, jnp.bfloat16
    vmem, dma = pltpu.VMEM, pltpu.SemaphoreType.DMA
    args = [pltpu.with_memory_space_constraint(x, pltpu.HBM) for x in args]
    out = pl.pallas_call(
        functools.partial(kernel, layers, planes),
        out_shape=jax.ShapeDtypeStruct((32, 128), f32),
        in_specs=[pl.BlockSpec(memory_space=pltpu.HBM)] * 10,
        out_specs=pl.BlockSpec(memory_space=pltpu.VMEM),
        scratch_shapes=[vmem(a.shape, a.dtype) for a in args]
        + [
            vmem((OWN_ROWS * 32, WIDE), bf16), vmem((144, WIDE), bf16),
            vmem((4, WIDE, elems), bf16), vmem((4, 32, elems), f32), vmem((4, elems), jnp.int32), vmem((8, elems), f32),
            vmem((3, 4, elems), bf16), vmem((3, 4, elems), bf16),
            vmem((64, WIDE), bf16), vmem((64, WIDE), bf16),
            vmem((4, 32, 128), bf16), vmem((4, 32, 128), bf16),
            vmem((4, 16, 128), bf16), vmem((4, 16, 128), bf16),
            vmem((8, elems), f32), vmem((8, elems), f32),
            vmem((layers, 2 * per, WIDE), f32), vmem((layers, 2 * per, WIDE), f32),
            vmem((layers, per, WIDE), f32), vmem((layers, per, WIDE), f32),
            vmem((1, elems), f32), vmem((1, elems), f32),
            vmem((4, 1, 128), f32), vmem((2, 4, 1, 128), f32),
            vmem((2, 16, 128), f32), vmem((16, 128), f32), vmem((layers // 2, 16, 128), f32), vmem((2, 16, 128), f32),
            dma((10,)), dma, dma, dma((3,)), dma((3,)), dma((4,)), dma((4,)), dma((4,)), dma((4,)),
        ]
        + [dma((layers,)), dma((layers,)), dma((layers,)), dma((layers,)), dma((2, 4)), dma((2, 4)), dma, dma]
        + [dma((layers // 2,)), dma((layers // 2,)), dma, dma],
        compiler_params=pltpu.CompilerParams(collective_id=0, has_side_effects=True, vmem_limit_bytes=40 << 20),
        name="ice_gradient",
    )(*args)
    return out.reshape(4096)


def solution(mesh):
    return jax.shard_map(
        functools.partial(shards, mesh.shape["layer"], mesh.shape["plane"]),
        mesh=mesh,
        in_specs=(
            P(None, "layer", "plane"),
            P(None, "layer", "plane"),
            P(None, "plane"),
            P(None, "plane"),
            P(None, "plane"),
            P(None, "plane"),
            P("layer", "plane"),
            P("layer", "plane"),
            P("layer", "plane"),
            P("layer", "plane"),
        ),
        out_specs=P("plane"),
        check_vma=False,
    )
```
